32 devices in a mesh: dp: 8 (over y, x, core), row: 2 (over z_hi), col: 2 (over z_lo).
Axes of the slice: x: 2, y: 2, z: 4 (z_hi: 2, z_lo: 2; z = z_hi * 2 + z_lo), core: 2. Of those that a mesh axis runs over, the one named last changes fastest.
Arguments:
- tokens: bfloat16 [8, 512, 2048], P('dp', 'col', 'row'), as said below
- segments: int32 [8, 512], P('dp'), may hold values from 0 to 3, as said below
- positions: int32 [8, 512], P('dp'), may hold values from 0 to 255, as said below
- attn_gain: float32 [2048], P('row'), may hold values from 0.5 to 1.5
- w_query: bfloat16 [2048, 2048], P('row', 'col'), as said below
- w_key: bfloat16 [2048, 256], P('row', 'col'), as said below
- w_value: bfloat16 [2048, 256], P('row', 'col'), may hold values from -0.125 to 0.125
- w_out: bfloat16 [2048, 2048], P('col', 'row'), may hold values from -0.5 to 0.5
- mlp_gain: float32 [2048], P('row'), may hold values from 0.5 to 1.5
- w_gate: bfloat16 [2048, 5632], P('row', 'col'), may hold values from -0.125 to 0.125
- w_up: bfloat16 [2048, 5632], P('row', 'col'), as said below
- w_down: bfloat16 [5632, 2048], P('col', 'row'), as said below
- cotangent: bfloat16 [8, 512, 2048], P('dp', 'col', 'row'), as said below
Outputs:
- out: bfloat16 [8, 512, 2048], P('dp', 'col', 'row')
- grad_tokens: bfloat16 [8, 512, 2048], P('dp', 'col', 'row')
- grad_attn_gain: float32 [2048], P('row')
- grad_query: float32 [2, 1024, 2048], P('row', 'dp', 'col')
- grad_key: float32 [2, 1024, 256], P('row', 'dp', 'col')
- grad_value: float32 [2, 1024, 256], P('row', 'dp', 'col')
- grad_out: float32 [2, 1024, 2048], P('col', 'dp', 'row')
- grad_mlp_gain: float32 [2048], P('row')
- grad_gate: float32 [2, 1024, 5632], P('row', 'dp', 'col')
- grad_up: float32 [2, 1024, 5632], P('row', 'dp', 'col')
- grad_down: float32 [2, 2816, 2048], P('col', 'dp', 'row')
The draws below stay inside these ranges and needn't reach their ends.
Inputs may be any that keep to these rules, and one draw needn't show every extreme that they name: `segments`: document numbers never fall along a sequence, start at 0, and every sequence holds exactly 4 documents. `positions`: a token's position within its document: 0 at its first token, rising by one; the longest document of every sequence has 256 tokens. `tokens`: activations. `w_query`: a projection matrix. `w_key`: a projection matrix. `w_up`: a projection matrix. `w_down`: a projection matrix. `cotangent`: gradients.
All inputs are finite; a program needn't handle non-finite values.
Results may differ from the reference program's by a relative error of at most 0.02.
Values may be sent and summed in bfloat16 or wider, within the bound.
No kernel may reach another device: no remote copies, remote signals or barrier semaphores. Data moves between devices by JAX's collectives and lax.ppermute only.
A program may use at most 192 MiB of HBM per device.

```python
import jax
import jax.numpy as jnp
from jax import lax

D = 2048
HQ = 32
KV = 4
HD = 64
FF = 5632
SEQ = 512
DOCS = 4
SEQS = 8
N_ROW = 2
N_COL = 2


def token_parts(key):
    base_key, row_key, col_key = jax.random.split(key, 3)
    ramp_place = jnp.arange(D, dtype=jnp.float32) / (D - 1.0)
    base = jax.random.normal(base_key, (SEQS, SEQ, D), jnp.float32)
    ramp = -1.2 + 2.4 * ramp_place
    row_scale = jnp.exp(jax.random.uniform(row_key, (SEQS, SEQ, 1), jnp.float32, -1.2, 1.2))
    col_scale = jnp.exp(ramp + jax.random.uniform(col_key, (D,), jnp.float32, -0.4, 0.4))
    return (base, row_scale, col_scale)


def draw_tokens(key, part):
    base, row_scale, col_scale = token_parts(key)
    return (base * row_scale * col_scale).astype(jnp.bfloat16)


def draw_cotangent(key, part):
    base, row_scale, col_scale = token_parts(key)
    noise_key = jax.random.fold_in(key, 31)
    noise = jnp.clip(jax.random.normal(noise_key, (SEQS, SEQ, D), jnp.float32), -6.0, 6.0)
    pattern = base * col_scale / 1.5
    return (0.8 * noise + 0.6 * pattern).astype(jnp.bfloat16)


def feed_forward_pair(key):
    up_key = jax.random.fold_in(key, 41)
    down_key = jax.random.fold_in(key, 42)
    up = jax.random.normal(up_key, (D, FF), jnp.float32) * D ** (-0.5)
    down_noise = jax.random.normal(down_key, (FF, D), jnp.float32) * FF ** (-0.5)
    down = 0.8660254 * down_noise + 0.5 * jnp.transpose(up) * (D / FF) ** 0.5
    return (up, down)


def draw_w_up(key, part):
    return feed_forward_pair(key)[0].astype(jnp.bfloat16)


def draw_w_down(key, part):
    return feed_forward_pair(key)[1].astype(jnp.bfloat16)


def drawn_projections(key):
    query_key = jax.random.fold_in(key, 11)
    other_key = jax.random.fold_in(key, 12)
    base = jax.random.normal(query_key, (D, HQ * HD), jnp.float32) * D ** (-0.5)
    other = jax.random.normal(other_key, (D, KV * HD), jnp.float32) * D ** (-0.5)
    return (base, other)


def draw_w_query(key, part):
    return drawn_projections(key)[0].astype(jnp.bfloat16)


def draw_w_key(key, part):
    return drawn_projections(key)[1].astype(jnp.bfloat16)


def document_layout(key):
    layout_key = jax.random.fold_in(key, 21)
    seq_keys = jax.random.split(layout_key, SEQS)
    longest = SEQ // 2
    remaining = SEQ - longest

    def one_sequence(seq_key):
        cut_key, place_key = jax.random.split(seq_key)
        cuts = jnp.sort(jax.random.permutation(cut_key, remaining - 1)[:DOCS - 2] + 1).astype(jnp.int32)
        bounds = jnp.concatenate([jnp.zeros((1,), jnp.int32), cuts, jnp.full((1,), remaining, jnp.int32)])
        pieces = (bounds[1:] - bounds[:-1]).astype(jnp.int32)
        chosen = jax.random.randint(place_key, (), 0, DOCS).astype(jnp.int32)
        order = jnp.arange(DOCS, dtype=jnp.int32)
        before = pieces[jnp.clip(order, 0, DOCS - 2)]
        after = pieces[jnp.clip(order - 1, 0, DOCS - 2)]
        lengths = jnp.where(order < chosen, before, jnp.where(order == chosen, longest, after)).astype(jnp.int32)
        starts = (jnp.cumsum(lengths) - lengths).astype(jnp.int32)
        places = jnp.arange(SEQ, dtype=jnp.int32)
        passed = places[:, None] >= starts[None, 1:]
        numbers = jnp.sum(passed.astype(jnp.int32), axis=1).astype(jnp.int32)
        begins = jnp.max(jnp.where(places[:, None] >= starts[None, :], starts[None, :], 0), axis=1)
        return (numbers, (places - begins).astype(jnp.int32))
    return jax.vmap(one_sequence)(seq_keys)


def draw_segments(key, part):
    return document_layout(key)[0]


def draw_positions(key, part):
    return document_layout(key)[1]


def block_levels(rng, extent, shards, smallest, largest):
    def one(dim, parts):
        draws = jax.random.uniform(jax.random.fold_in(jax.random.fold_in(rng, 6), dim), (parts,), jnp.float32, smallest / len(shards), largest / len(shards))
        return jnp.repeat(jnp.exp(draws), extent[dim] // parts).reshape((-1,) + (1,) * (len(extent) - dim - 1))

    gain = one(*shards[0])
    for cut in shards[1:]:
        gain = gain * one(*cut)
    return gain


def gaussian(key, shape, width, bound, cuts=(), kind=jnp.bfloat16):
    drawn = width * jax.random.normal(key, shape, jnp.float32)
    if cuts:
        drawn = drawn * block_levels(key, shape, cuts, -0.22, 0.18)
    return jnp.clip(drawn, -bound, bound).astype(kind)


def setup_inputs(seed: int = 0) -> dict:
    seeds = jax.random.split(jax.random.key(seed), 14)
    tokens = draw_tokens(jax.random.fold_in(seeds[13], 71), 0)
    segments = draw_segments(jax.random.fold_in(seeds[13], 71), 0)
    positions = draw_positions(jax.random.fold_in(seeds[13], 71), 0)
    attn_gain = jnp.clip(1.0 + 0.1 * jax.random.normal(seeds[3], (D,), jnp.float32), 0.5, 1.5)
    w_query = draw_w_query(jax.random.fold_in(seeds[13], 71), 0)
    w_key = draw_w_key(jax.random.fold_in(seeds[13], 71), 0)
    w_value = gaussian(seeds[6], (D, KV * HD), D ** -0.5, 0.125, ((0, 2), (1, 2)))
    w_out = gaussian(seeds[7], (HQ * HD, D), (HQ * HD // 16) ** -0.5, 0.5, ((0, 2), (1, 2)))
    mlp_gain = jnp.clip(1.0 + 0.1 * jax.random.normal(seeds[8], (D,), jnp.float32), 0.5, 1.5)
    w_gate = gaussian(seeds[9], (D, FF), D ** -0.5, 0.125, ((0, 2), (1, 2)))
    w_up = draw_w_up(jax.random.fold_in(seeds[13], 71), 0)
    w_down = draw_w_down(jax.random.fold_in(seeds[13], 71), 0)
    cotangent = draw_cotangent(jax.random.fold_in(seeds[13], 71), 0)
    return dict(tokens=tokens, segments=segments, positions=positions, attn_gain=attn_gain, w_query=w_query, w_key=w_key, w_value=w_value, w_out=w_out, mlp_gain=mlp_gain, w_gate=w_gate, w_up=w_up, w_down=w_down, cotangent=cotangent)


epsilon = 1e-05
masked_score = -1e+30
highest = lax.Precision.HIGHEST

@jax.custom_vjp
def low(v):
    return lax.optimization_barrier(v.astype(jnp.bfloat16)).astype(jnp.float32)

@jax.custom_vjp
def low_back(v):
    return v

def low_keep(v):
    return (low(v), None)

def low_pass(kept, grad):
    return (grad,)

def back_keep(v):
    return (v, None)

def back_low(kept, grad):
    return (low(grad),)
low.defvjp(low_keep, low_pass)
low_back.defvjp(back_keep, back_low)

def rotary(values, token_pos):
    head_dim = values.shape[-1]
    half_dim = head_dim // 2
    frequency = 10000.0 ** (-jnp.arange(half_dim, dtype=jnp.float32) * 2.0 / head_dim)
    angles = token_pos.astype(jnp.float32)[:, None] * frequency[None, :]
    cosine_table = jnp.cos(angles)[:, None, :]
    sine_table = jnp.sin(angles)[:, None, :]
    lower_half = values[..., :half_dim]
    upper_half = values[..., half_dim:]
    return jnp.concatenate([lower_half * cosine_table - upper_half * sine_table, upper_half * cosine_table + lower_half * sine_table], axis=-1)

def attend(queries, keys_rot, values, segment_ids):
    length = queries.shape[0]
    block = min(512, length)
    score_scale = HD ** (-0.5)
    cols_index = jnp.arange(length, dtype=jnp.int32)

    def one_block(index):
        start = index * block
        query_part = lax.dynamic_slice_in_dim(queries, start, block, 0)
        rows_index = start + jnp.arange(block, dtype=jnp.int32)
        row_segments = lax.dynamic_slice_in_dim(segment_ids, start, block, 0)
        allowed = (rows_index[:, None] >= cols_index[None, :]) & (row_segments[:, None] == segment_ids[None, :])
        raw = low_back(jnp.einsum('bkgd,lkd->kgbl', query_part, keys_rot, precision=highest))
        scores = jnp.where(allowed, raw * score_scale, masked_score)
        probs = jax.nn.softmax(scores, axis=-1)
        return jnp.einsum('kgbl,lkd->bkgd', low(probs), values, precision=highest)
    outputs = lax.map(jax.checkpoint(one_block), jnp.arange(length // block, dtype=jnp.int32))
    return outputs.reshape(queries.shape)

def layer(inputs, segment_ids, token_pos, params):
    attn_gain, w_query, w_key, w_value, w_out, mlp_gain, w_gate, w_up, w_down = params
    length = inputs.shape[0]
    group_size = HQ // KV
    factor_one = lax.rsqrt(lax.optimization_barrier(jnp.mean(inputs * inputs, axis=-1, keepdims=True)) + epsilon)
    normed_one = low(inputs * factor_one * attn_gain)
    query_raw = low_back(jnp.dot(normed_one, w_query, precision=highest))
    key_raw = low_back(jnp.dot(normed_one, w_key, precision=highest))
    value_low = low(low_back(jnp.dot(normed_one, w_value, precision=highest)))
    query_low = low(rotary(query_raw.reshape(length, HQ, HD), token_pos)).reshape(length, KV, group_size, HD)
    key_low = low(rotary(key_raw.reshape(length, KV, HD), token_pos))
    attended = attend(query_low, key_low, value_low.reshape(length, KV, HD), segment_ids)
    attended_low = low(low_back(attended.reshape(length, HQ * HD)))
    hidden_state = inputs + low_back(jnp.dot(attended_low, w_out, precision=highest))
    factor_two = lax.rsqrt(lax.optimization_barrier(jnp.mean(hidden_state * hidden_state, axis=-1, keepdims=True)) + epsilon)
    normed_two = low(hidden_state * factor_two * mlp_gain)
    gate_part = low_back(jnp.dot(normed_two, w_gate, precision=highest))
    up_part = low_back(jnp.dot(normed_two, w_up, precision=highest))
    hidden_low = low(jax.nn.silu(gate_part) * up_part)
    return hidden_state + jnp.dot(hidden_low, w_down, precision=highest)

def reference(tokens, segments, positions, attn_gain, w_query, w_key, w_value, w_out, mlp_gain, w_gate, w_up, w_down, cotangent):
    params = tuple((array.astype(jnp.float32) for array in (attn_gain, w_query, w_key, w_value, w_out, mlp_gain, w_gate, w_up, w_down)))
    inputs = tokens.astype(jnp.float32)

    def whole(inputs, params):

        def step(carry, item):
            return (carry, jax.checkpoint(layer)(item[0], item[1], item[2], params))
        return lax.scan(step, jnp.zeros((), jnp.float32), (inputs, segments, positions))[1]
    outputs, pullback = jax.vjp(whole, inputs, params)
    grad_inputs, grad_params = pullback(cotangent.astype(jnp.float32))
    grad_query = grad_params[1].reshape(N_ROW, D // N_ROW, HQ * HD)
    grad_key = grad_params[2].reshape(N_ROW, D // N_ROW, KV * HD)
    grad_value = grad_params[3].reshape(N_ROW, D // N_ROW, KV * HD)
    grad_out = grad_params[4].reshape(N_COL, HQ * HD // N_COL, D)
    grad_gate = grad_params[6].reshape(N_ROW, D // N_ROW, FF)
    grad_up = grad_params[7].reshape(N_ROW, D // N_ROW, FF)
    grad_down = grad_params[8].reshape(N_COL, FF // N_COL, D)
    return (outputs.astype(jnp.bfloat16), grad_inputs.astype(jnp.bfloat16), grad_params[0], grad_query, grad_key, grad_value, grad_out, grad_params[5], grad_gate, grad_up, grad_down)
```

```python
import jax
import jax.numpy as jnp
from jax import lax
from jax.sharding import PartitionSpec as P

HD = 64
epsilon = 1e-05
masked_score = -1e30
f32 = jnp.float32
bf16 = jnp.bfloat16


def swap_core(v):
    n = lax.axis_size("dp")
    return lax.ppermute(v, "dp", [(i, i ^ 1) for i in range(n)])


def swap_chip(v, bit):
    n = lax.axis_size("dp")
    return lax.ppermute(v, "dp", [(i, i ^ (2 << bit)) for i in range(n)])


def swap_row(v):
    return lax.ppermute(v, "row", [(0, 1), (1, 0)])


def swap_col(v):
    return lax.ppermute(v, "col", [(0, 1), (1, 0)])


def side_perms():
    chips = lax.axis_size("dp") // 2
    first, second = [], []
    for e in range(chips):
        for a in range(2):
            same = (2 * e + a) * 2 + a
            other = (2 * e + a) * 2 + 1 - a
            mate = (2 * e + 1 - a) * 2 + a
            first += [(same, mate), (other, same)]
            second += [(other, mate)]
    return first, second


def flip(perm):
    return [(b, a) for a, b in perm]


def permute_side(v, perm):
    return lax.ppermute(v, ("dp", "row"), perm)


def xor_blocks(blocks, index):
    bit = 0
    while (1 << bit) < len(blocks):
        on = ((index >> bit) & 1) == 1
        blocks = [jnp.where(on, blocks[i ^ (1 << bit)], blocks[i]) for i in range(len(blocks))]
        bit += 1
    return blocks


def xor_axis(v, index, axis, count):
    return jnp.concatenate(xor_blocks(jnp.split(v, count, axis), index), axis)


def pick(v, index, axis):
    lo, hi = jnp.split(v, 2, axis)
    return jnp.where(index == 0, lo, hi)


def order_pair(mine, theirs, index, axis):
    return jnp.where(
        index == 0,
        jnp.concatenate([mine, theirs], axis),
        jnp.concatenate([theirs, mine], axis),
    )


def mm(a, b):
    return jnp.dot(a, b, preferred_element_type=f32)


def mm_t(a, b):
    return lax.dot_general(a, b, (((1,), (1,)), ((), ())), preferred_element_type=f32)


def t_mm(a, b):
    return lax.dot_general(a, b, (((0,), (0,)), ((), ())), preferred_element_type=f32)


def tp_gather(v):
    v = jnp.concatenate([v, swap_col(v)], 0)
    return jnp.concatenate([v, swap_core(v)], 0)


def tp_reduce(v):
    half = v.shape[0] // 2
    v = v[:half] + swap_core(v[half:].astype(bf16)).astype(f32)
    half = half // 2
    return v[:half] + swap_col(v[half:].astype(bf16)).astype(f32)


def gather_chips(shard, bits, axis):
    held = {0: shard}
    for bit in bits:
        keys = list(held)
        got = swap_chip(jnp.concatenate([held[j] for j in keys], axis), bit)
        for j, piece in zip(keys, jnp.split(got, len(keys), axis)):
            held[j ^ (1 << bit)] = piece
    return jnp.concatenate([held[j] for j in range(len(held))], axis)


def cut(v, start, size, axis):
    return lax.slice_in_dim(v, start, start + size, axis=axis)


def take_keys(v, have, want, axis):
    width = v.shape[axis] // (2 * len(have))
    out = []
    for h in range(2):
        for j in want:
            out.append(cut(v, (h * len(have) + have.index(j)) * width, width, axis))
    return out[0] if len(out) == 1 else jnp.concatenate(out, axis)


def reduce_features(make, bits, axis):
    count = 1 << len(bits)
    keys = list(range(count))
    got = []

    def total(want):
        value = make(want)
        for have, arr in got:
            value = value + take_keys(arr, have, want, axis).astype(f32)
        return value

    for bit in bits:
        send = [j for j in keys if (j >> bit) & 1]
        keys = [j for j in keys if not (j >> bit) & 1]
        arr = swap_chip(total(send).astype(bf16), bit)
        got.append(([j ^ (1 << bit) for j in send], arr))
    own, other = jnp.split(total(keys), 2, axis)
    return own + swap_row(other.astype(bf16)).astype(f32)


def rotary(values, cosine, sine):
    half = HD // 2
    lower = values[..., :half]
    upper = values[..., half:]
    return jnp.concatenate([lower * cosine - upper * sine, upper * cosine + lower * sine], -1)


def on_device(
    tokens,
    segments,
    positions,
    attn_gain,
    w_query,
    w_key,
    w_value,
    w_out,
    mlp_gain,
    w_gate,
    w_up,
    w_down,
    cotangent,
):
    dp = lax.axis_index("dp")
    e, k = dp >> 1, dp & 1
    r, c = lax.axis_index("row"), lax.axis_index("col")
    chips = lax.axis_size("dp") // 2
    nbits = chips.bit_length() - 1
    x_first = list(range(nbits))
    y_first = x_first[::-1]
    diag = k == r
    length = segments.shape[1]
    blk = length // 4
    dh = tokens.shape[2]
    D = 2 * dh
    fw = dh // chips
    first, second = side_perms()

    def spread_in(v):
        parts = v[0].reshape(2, blk, dh)
        here = jnp.where(r == 0, parts[0], parts[1])
        away = jnp.where(r == 0, parts[1], parts[0])
        got_a = permute_side(away, first)
        got_b = permute_side(here, second)
        own = jnp.where(diag, here, got_a)
        oth = jnp.where(diag, got_a, got_b)
        return jnp.concatenate([xor_axis(own, e, 1, chips), xor_axis(oth, e, 1, chips)], 1)

    def spread_out(v):
        own = xor_axis(v[:, :dh], e, 1, chips)
        oth = xor_axis(v[:, dh:], e, 1, chips)
        got_a = permute_side(jnp.where(diag, oth, own), flip(first))
        got_b = permute_side(oth, flip(second))
        here = jnp.where(diag, own, got_b)
        return order_pair(here, got_a, r, 0)[None]

    gains = jnp.stack([attn_gain, mlp_gain])
    gains = jnp.concatenate(
        [xor_axis(gains, e, 1, chips), xor_axis(swap_row(gains), e, 1, chips)], 1
    )
    meta = jnp.concatenate([segments, positions], 0)
    meta = jnp.where(diag, meta, swap_core(meta))
    place = jnp.arange(length, dtype=jnp.int32)[None]
    meta = jnp.concatenate([meta, place], 0)
    quarter = jnp.split(meta, 4, 1)
    meta = jnp.concatenate(
        xor_blocks([quarter[0], quarter[2], quarter[1], quarter[3]], 2 * k + c), 1
    )
    seg, pos, place = meta[0], meta[1], meta[2]

    def own_rows(w):
        return xor_axis(pick(w, k, 1), e, 0, chips)

    def own_cols(w):
        return xor_axis(pick(w, k, 0), e, 1, chips)

    x = spread_in(tokens)
    wq = jnp.concatenate([own_rows(w_query), own_rows(w_key), own_rows(w_value)], 1)
    wq_oth = gather_chips(swap_row(wq[:fw]), x_first, 0)
    w_qkv = jnp.concatenate([wq, wq_oth], 0)
    wo = own_cols(w_out)
    wo_oth = gather_chips(swap_row(wo[:, :fw]), y_first, 1)
    w_o = jnp.concatenate([wo, wo_oth], 1)
    g = spread_in(cotangent)

    hidden = w_gate.shape[1] // 2
    unit = 128
    n0 = (hidden // unit + 1) // 2 * unit
    spans = [(0, n0), (n0, hidden)]
    wg_own, wu_own, wd_own = own_rows(w_gate), own_rows(w_up), own_cols(w_down)
    chunks = []
    for lo, hi in spans:
        pg, pu, pd = wg_own[:, lo:hi], wu_own[:, lo:hi], wd_own[lo:hi]
        sg = swap_row(pg[:fw])
        su = swap_row(pu[:fw])
        sd = swap_row(pd[:, :fw])
        mid = (hi - lo) // 2
        og = gather_chips(sg, x_first, 0)
        ou = gather_chips(su, y_first, 0)
        od = jnp.concatenate(
            [gather_chips(sd[:mid], x_first, 1), gather_chips(sd[mid:], y_first, 1)], 0
        )
        chunks.append(
            (
                jnp.concatenate([pg, og], 0),
                jnp.concatenate([pu, ou], 0),
                jnp.concatenate([pd, od], 1),
            )
        )

    xf = x.astype(f32)
    r1 = lax.rsqrt(jnp.sum(xf * xf, axis=1, keepdims=True) / D + epsilon)
    a1 = tp_gather((xf * r1 * gains[0]).astype(bf16))
    qkv = mm(a1, w_qkv)
    nq = w_query.shape[1] // 2
    heads = nq // HD
    half = HD // 2
    frequency = 10000.0 ** (-jnp.arange(half, dtype=f32) * 2.0 / HD)
    angles = pos.astype(f32)[:, None] * frequency[None, :]
    cosine, sine = jnp.cos(angles), jnp.sin(angles)
    scale = HD ** (-0.5)
    q = rotary(qkv[:, :nq].reshape(length, heads, HD), cosine[:, None], sine[:, None]).astype(bf16)
    kk = rotary(qkv[:, nq : nq + HD], cosine, sine).astype(bf16)
    vv = qkv[:, nq + HD :].astype(bf16)
    allowed = (place[:, None] >= place[None, :]) & (seg[:, None] == seg[None, :])

    def probabilities():
        raw = jnp.einsum("bhd,ld->hbl", q, kk, preferred_element_type=f32)
        scores = jnp.where(allowed, raw * scale, masked_score)
        top = jnp.max(scores, axis=-1, keepdims=True)
        weights = jnp.exp(scores - top)
        return weights / jnp.sum(weights, axis=-1, keepdims=True)

    probs = probabilities()
    o = jnp.einsum("hbl,ld->bhd", probs.astype(bf16), vv, preferred_element_type=f32)
    o = o.astype(bf16).reshape(length, nq)
    hres = xf + tp_reduce(mm(o, w_o))
    r2 = lax.rsqrt(jnp.sum(hres * hres, axis=1, keepdims=True) / D + epsilon)
    a2 = tp_gather((hres * r2 * gains[1]).astype(bf16))
    g_all = tp_gather(g)

    def row_pieces(v, keys):
        return take_keys(v, list(range(chips)), keys, 1)

    out_part, da2_part = None, None
    ms, gate_grads, up_grads = [], [], []
    for wg, wu, wd in chunks:
        gate, up, dm = mm(a2, wg), mm(a2, wu), mm_t(g_all, wd)
        sig = jax.nn.sigmoid(gate)
        act = gate * sig
        m = (act * up).astype(bf16)
        dgate = (dm * up * sig * (1.0 + gate * (1.0 - sig))).astype(bf16)
        dup = (dm * act).astype(bf16)
        ms.append(m)
        part = mm(m, wd)
        out_part = part if out_part is None else out_part + part
        part = mm_t(dgate, wg) + mm_t(dup, wu)
        da2_part = part if da2_part is None else da2_part + part
        gate_grads.append(
            reduce_features(lambda ks, y=dgate: t_mm(row_pieces(a2, ks), y), x_first, 0)
        )
        up_grads.append(
            reduce_features(lambda ks, y=dup: t_mm(row_pieces(a2, ks), y), y_first, 0)
        )
    m_all = jnp.concatenate(ms, 1)
    mid = hidden // 2
    down_lo = reduce_features(lambda ks: t_mm(m_all[:, :mid], row_pieces(g_all, ks)), x_first, 1)
    down_hi = reduce_features(lambda ks: t_mm(m_all[:, mid:], row_pieces(g_all, ks)), y_first, 1)
    result = spread_out((hres + tp_reduce(out_part)).astype(bf16))

    def norm_back(inputs, factor, gain, upstream):
        weighted = upstream * gain
        dotted = jnp.sum(weighted * inputs, axis=1, keepdims=True)
        grad = factor * weighted - inputs * factor**3 * dotted / D
        return grad, jnp.sum(upstream * inputs * factor, axis=0)

    dh_grad, gain_two = norm_back(hres, r2, gains[1], tp_reduce(da2_part))
    dh_grad = dh_grad + g.astype(f32)
    dz = tp_gather(dh_grad.astype(bf16))
    do = mm_t(dz, w_o).astype(bf16).reshape(length, heads, HD)
    out_sum = reduce_features(lambda ks: t_mm(o, row_pieces(dz, ks)), x_first, 1)

    dv = jnp.einsum("hbl,bhd->ld", probs.astype(bf16), do, preferred_element_type=f32)
    dprob = jnp.einsum("bhd,ld->hbl", do, vv, preferred_element_type=f32)
    centre = jnp.sum(probs * dprob, axis=-1, keepdims=True)
    ds = (probs * (dprob - centre) * scale).astype(bf16)
    dq = jnp.einsum("hbl,ld->bhd", ds, kk, preferred_element_type=f32)
    dk = jnp.einsum("hbl,bhd->ld", ds, q, preferred_element_type=f32)
    dq = rotary(dq, cosine[:, None], -sine[:, None]).reshape(length, nq)
    dk = rotary(dk, cosine, -sine)
    dqkv = jnp.concatenate([dq, dk, dv], 1).astype(bf16)
    da1 = tp_reduce(mm_t(dqkv, w_qkv))
    qkv_sum = reduce_features(lambda ks: t_mm(row_pieces(a1, ks), dqkv), y_first, 0)
    grad_x, gain_one = norm_back(xf, r1, gains[0], da1)
    grad_x = spread_out((grad_x + dh_grad).astype(bf16))

    both = jnp.stack([gain_one, gain_two])
    own = xor_axis(both[:, :dh], e, 1, chips)
    oth = xor_axis(both[:, dh:], e, 1, chips)
    own = own + swap_row(oth)
    own = own + swap_col(own)
    own = own + swap_core(own)
    for bit in x_first:
        own = own + swap_chip(own, bit)

    def rows_home(v):
        mine, theirs = pick(v, k, 0), pick(v, 1 - k, 0)
        return mine, swap_core(theirs)

    gate_up = jnp.concatenate(gate_grads + up_grads, 1)
    mine, theirs = rows_home(gate_up)
    grad_gate = order_pair(mine[:, :hidden], theirs[:, :hidden], k, 1)
    grad_up = order_pair(mine[:, hidden:], theirs[:, hidden:], k, 1)
    mine, theirs = rows_home(qkv_sum)
    grad_query = order_pair(mine[:, :nq], theirs[:, :nq], k, 1)
    grad_key = order_pair(mine[:, nq : nq + HD], theirs[:, nq : nq + HD], k, 1)
    grad_value = order_pair(mine[:, nq + HD :], theirs[:, nq + HD :], k, 1)

    def exchange(v):
        rows = v.shape[0] // chips
        view = v.reshape(chips // 2, 2, rows, v.shape[1]).astype(bf16)
        mine = jnp.where(k == 0, view[:, 0], view[:, 1])
        got = swap_core(jnp.where(k == 0, view[:, 1], view[:, 0]))
        full = order_pair(mine, got, k, 0)
        rel = xor_blocks([full[i] for i in range(chips)], e)
        n = lax.axis_size("dp")
        out = [rel[0]]
        for j in range(1, chips):
            out.append(lax.ppermute(rel[j], "dp", [(i, i ^ (2 * j)) for i in range(n)]))
        return jnp.concatenate(xor_blocks(out, e), 1).astype(f32)

    grad_down = exchange(jnp.concatenate([down_lo, down_hi], 0))
    grad_out = exchange(out_sum)
    return (
        result,
        grad_x,
        own[0],
        grad_query[None],
        grad_key[None],
        grad_value[None],
        grad_out[None],
        own[1],
        grad_gate[None],
        grad_up[None],
        grad_down[None],
    )


def solution(mesh):
    placed = (
        P("dp", "col", "row"),
        P("dp", None),
        P("dp", None),
        P("row"),
        P("row", "col"),
        P("row", "col"),
        P("row", "col"),
        P("col", "row"),
        P("row"),
        P("row", "col"),
        P("row", "col"),
        P("col", "row"),
        P("dp", "col", "row"),
    )
    return jax.shard_map(
        on_device,
        mesh=mesh,
        in_specs=placed,
        out_specs=(
            P("dp", "col", "row"),
            P("dp", "col", "row"),
            P("row"),
            P("row", "dp", "col"),
            P("row", "dp", "col"),
            P("row", "dp", "col"),
            P("col", "dp", "row"),
            P("row"),
            P("row", "dp", "col"),
            P("row", "dp", "col"),
            P("col", "dp", "row"),
        ),
        check_vma=False,
    )
```

```python
import jax
import jax.numpy as jnp
from jax import lax
from jax.experimental import pallas as pl
from jax.experimental.pallas import tpu as pltpu
from jax.sharding import PartitionSpec as P

HD = 64
epsilon = 1e-05
masked_score = -1e30
f32 = jnp.float32
bf16 = jnp.bfloat16


def swap_core(v):
    n = lax.axis_size("dp")
    return lax.ppermute(v, "dp", [(i, i ^ 1) for i in range(n)])


def swap_chip(v, bit):
    n = lax.axis_size("dp")
    return lax.ppermute(v, "dp", [(i, i ^ (2 << bit)) for i in range(n)])


def swap_row(v):
    return lax.ppermute(v, "row", [(0, 1), (1, 0)])


def swap_col(v):
    return lax.ppermute(v, "col", [(0, 1), (1, 0)])


def side_perms():
    chips = lax.axis_size("dp") // 2
    first, second = [], []
    for e in range(chips):
        for a in range(2):
            same = (2 * e + a) * 2 + a
            other = (2 * e + a) * 2 + 1 - a
            mate = (2 * e + 1 - a) * 2 + a
            first += [(same, mate), (other, same)]
            second += [(other, mate)]
    return first, second


def flip(perm):
    return [(b, a) for a, b in perm]


def permute_side(v, perm):
    return lax.ppermute(v, ("dp", "row"), perm)


def xor_blocks(blocks, index):
    bit = 0
    while (1 << bit) < len(blocks):
        on = ((index >> bit) & 1) == 1
        blocks = [jnp.where(on, blocks[i ^ (1 << bit)], blocks[i]) for i in range(len(blocks))]
        bit += 1
    return blocks


def xor_axis(v, index, axis, count):
    return jnp.concatenate(xor_blocks(jnp.split(v, count, axis), index), axis)


def pick(v, index, axis):
    lo, hi = jnp.split(v, 2, axis)
    return jnp.where(index == 0, lo, hi)


def order_pair(mine, theirs, index, axis):
    return jnp.where(
        index == 0,
        jnp.concatenate([mine, theirs], axis),
        jnp.concatenate([theirs, mine], axis),
    )


def mm(a, b):
    return jnp.dot(a, b, preferred_element_type=f32)


def mm_t(a, b):
    return lax.dot_general(a, b, (((1,), (1,)), ((), ())), preferred_element_type=f32)


def t_mm(a, b):
    return lax.dot_general(a, b, (((0,), (0,)), ((), ())), preferred_element_type=f32)


def tp_gather(v):
    v = jnp.concatenate([v, swap_col(v)], 0)
    return jnp.concatenate([v, swap_core(v)], 0)


def tp_reduce(v):
    half = v.shape[0] // 2
    v = v[:half] + swap_core(v[half:].astype(bf16)).astype(f32)
    half = half // 2
    return v[:half] + swap_col(v[half:].astype(bf16)).astype(f32)


def gather_chips(shard, bits, axis):
    held = {0: shard}
    for bit in bits:
        keys = list(held)
        got = swap_chip(jnp.concatenate([held[j] for j in keys], axis), bit)
        for j, piece in zip(keys, jnp.split(got, len(keys), axis)):
            held[j ^ (1 << bit)] = piece
    return jnp.concatenate([held[j] for j in range(len(held))], axis)


def cut(v, start, size, axis):
    return lax.slice_in_dim(v, start, start + size, axis=axis)


def take_keys(v, have, want, axis):
    width = v.shape[axis] // (2 * len(have))
    out = []
    for h in range(2):
        for j in want:
            out.append(cut(v, (h * len(have) + have.index(j)) * width, width, axis))
    return out[0] if len(out) == 1 else jnp.concatenate(out, axis)


def reduce_features(make, bits, axis):
    count = 1 << len(bits)
    keys = list(range(count))
    got = []

    def total(want):
        value = make(want)
        for have, arr in got:
            value = value + take_keys(arr, have, want, axis).astype(f32)
        return value

    for bit in bits:
        send = [j for j in keys if (j >> bit) & 1]
        keys = [j for j in keys if not (j >> bit) & 1]
        arr = swap_chip(total(send).astype(bf16), bit)
        got.append(([j ^ (1 << bit) for j in send], arr))
    own, other = jnp.split(total(keys), 2, axis)
    return own + swap_row(other.astype(bf16)).astype(f32)


ANY = pl.BlockSpec(memory_space=pl.ANY)
LIMIT = 60 << 20


def params(dims):
    return pltpu.CompilerParams(
        dimension_semantics=("arbitrary",) * dims, vmem_limit_bytes=LIMIT
    )


def gather_unit(shard, first_cols):
    chips = lax.axis_size("dp") // 2
    rows, cols = shard.shape
    if chips == 4:
        got_x, got_y = swap_chip(shard, 0), swap_chip(shard, 1)
        far_a = swap_chip(got_x[:, :first_cols], 1)
        far_b = swap_chip(got_y[:, first_cols:], 0)
        return [
            (shard, 0, 0, 0, cols, 0),
            (got_x, 0, 1, 0, cols, 0),
            (got_y, 0, 2, 0, cols, 0),
            (far_a, 0, 3, 0, first_cols, 0),
            (far_b, 0, 3, 0, cols - first_cols, first_cols),
        ]
    nbits = chips.bit_length() - 1
    whole = gather_chips(shard, list(range(nbits)), 0)
    return [(whole, j * rows, j, 0, cols, 0) for j in range(chips)]


def clip_pieces(pieces, lo, hi):
    out = []
    for array, row, j, col, count, at in pieces:
        a, b = max(lo, at), min(hi, at + count)
        if a < b:
            out.append((array, row, j, col + a - at, b - a, a - lo))
    return out


def unique_arrays(pieces):
    arrays = []
    for piece in pieces:
        if not any(piece[0] is a for a in arrays):
            arrays.append(piece[0])
    return arrays


def piece_copies(pieces, arrays, refs, target, e, fw, sem):
    copies = []
    for array, row, j, col, count, at in pieces:
        ref = refs[[a is array for a in arrays].index(True)]
        copies.append(
            pltpu.make_async_copy(
                ref.at[pl.ds(row, fw), pl.ds(col, count)],
                target.at[pl.ds(pl.multiple_of((e ^ j) * fw, fw), fw), pl.ds(at, count)],
                sem,
            )
        )
    return copies


def start_all(copies):
    for copy in copies:
        copy.start()


def wait_all(copies):
    for copy in copies:
        copy.wait()


def lanes_low(shape):
    return lax.broadcasted_iota(jnp.int32, shape, 1) % 128 < HD


def turn(x, cosine, sine):
    lane = lax.broadcasted_iota(jnp.int32, x.shape, 1) % HD
    mate = jnp.where(lane < HD // 2, pltpu.roll(x, 128 - HD // 2, 1), pltpu.roll(x, HD // 2, 1))
    return x * cosine + mate * sine


def softmax_rows(qm, kdup, bias, scale):
    scores = mm_t(qm, kdup) * scale + bias
    top = jnp.max(scores, axis=1, keepdims=True)
    weights = jnp.exp(scores - top)
    return weights * (1.0 / jnp.sum(weights, axis=1, keepdims=True))


def split_store(value, send_ref, keep_ref, cols):
    half = value.shape[0] // 2
    keep_ref[:, cols] = value[:half]
    send_ref[:, cols] = value[half:].astype(bf16)


ROWS = 256


def attend_forward(scal, a1, w_query, wkv, w_out, pieces, cosine, sine, marks, marks_t):
    length, D = a1.shape
    dh = w_query.shape[0]
    nq = w_query.shape[1] // 2
    pairs = nq // 128
    fw = dh // (lax.axis_size("dp") // 2)
    qkv_pieces = clip_pieces(pieces, 0, nq + 128)
    out_pieces = clip_pieces(pieces, nq + 128, 2 * nq + 128)
    arrays = unique_arrays(pieces)
    scale = HD ** (-0.5)
    rows = min(ROWS, length)

    def kernel(scal_ref, a_ref, wq_ref, wkv_ref, wo_ref, cos_ref, sin_ref, mk_ref, mt_ref, *rest):
        piece_refs = rest[: len(arrays)]
        q_ref, kdup_ref, vdup_ref, o_ref, send_ref, keep_ref = rest[len(arrays) : len(arrays) + 6]
        wq, woth, wo, wot, qkv, bias, attended, sems = rest[len(arrays) + 6 :]
        e, k = scal_ref[0], scal_ref[1]
        step = pl.program_id(0)

        def first_copies():
            own = pltpu.make_async_copy(
                wq_ref.at[:, pl.ds(pl.multiple_of(k * nq, nq), nq)], wq, sems.at[0]
            )
            return [own] + piece_copies(qkv_pieces, arrays, piece_refs, woth, e, fw, sems.at[1])

        def later_copies():
            own = pltpu.make_async_copy(
                wo_ref.at[pl.ds(pl.multiple_of(k * nq, nq), nq), :], wo, sems.at[2]
            )
            return [own] + piece_copies(out_pieces, arrays, piece_refs, wot, e, fw, sems.at[3])

        @pl.when(step == 0)
        def _():
            copies = first_copies()
            start_all(copies)
            start_all(later_copies())
            same = mk_ref[:, 0:1] == mt_ref[0:1, :]
            before = mk_ref[:, 1:2] >= mt_ref[1:2, :]
            bias[...] = jnp.where(same & before, 0.0, masked_score)
            wait_all(copies)
            a_own, a_oth = a_ref[:, :dh], a_ref[:, dh:]
            qkv[:, :nq] = mm(a_own, wq[...]) + mm(a_oth, woth[:, :nq])
            kv = mm(a_own, wkv_ref[...]) + mm(a_oth, woth[:, nq:])
            low = lanes_low(kv.shape)
            kv = jnp.where(low, turn(kv, cos_ref[...], sin_ref[...]), kv)
            swapped = pltpu.roll(kv, HD, 1)
            kdup_ref[...] = jnp.where(low, kv, swapped).astype(bf16)
            vdup_ref[...] = jnp.where(low, swapped, kv).astype(bf16)

        at = pl.ds(pl.multiple_of(step * 128, 128), 128)
        q = turn(qkv[:, at], cos_ref[...], sin_ref[...]).astype(bf16)
        q_ref[...] = q
        kdup, vdup = kdup_ref[...], vdup_ref[...]
        low = lanes_low((rows, 128))
        zero = jnp.zeros((rows, 128), bf16)
        for lo in range(0, length, rows):
            part = q[lo : lo + rows]
            mask = bias[lo : lo + rows, :]
            outs = []
            for qm in (jnp.where(low, part, zero), jnp.where(low, zero, part)):
                probs = softmax_rows(qm, kdup, mask, scale).astype(bf16)
                outs.append(mm(probs, vdup))
            value = jnp.where(low, outs[0], outs[1]).astype(bf16)
            o_ref[lo : lo + rows, :] = value
            attended[lo : lo + rows, at] = value

        @pl.when(step == pairs - 1)
        def _():
            wait_all(later_copies())
            o = attended[...]
            split_store(mm(o, wo[...]), send_ref, keep_ref, slice(0, dh))
            split_store(mm_t(o, wot[...]), send_ref, keep_ref, slice(dh, D))

    full = lambda shape: pl.BlockSpec(shape, lambda i, s: (0,) * len(shape))
    return pl.pallas_call(
        kernel,
        grid_spec=pltpu.PrefetchScalarGridSpec(
            num_scalar_prefetch=1,
            grid=(pairs,),
            in_specs=[full(a1.shape), ANY, full(wkv.shape), ANY]
            + [full(v.shape) for v in (cosine, sine, marks, marks_t)]
            + [ANY] * len(arrays),
            out_specs=[
                pl.BlockSpec((length, 128), lambda i, s: (0, i)),
                full((length, 128)),
                full((length, 128)),
                pl.BlockSpec((length, 128), lambda i, s: (0, i)),
                full((length // 2, D)),
                full((length // 2, D)),
            ],
            scratch_shapes=[
                pltpu.VMEM((dh, nq), bf16),
                pltpu.VMEM((dh, nq + 128), bf16),
                pltpu.VMEM((nq, dh), bf16),
                pltpu.VMEM((dh, nq), bf16),
                pltpu.VMEM((length, nq), f32),
                pltpu.VMEM((length, length), f32),
                pltpu.VMEM((length, nq), bf16),
                pltpu.SemaphoreType.DMA((4,)),
            ],
        ),
        out_shape=[
            jax.ShapeDtypeStruct((length, nq), bf16),
            jax.ShapeDtypeStruct((length, 128), bf16),
            jax.ShapeDtypeStruct((length, 128), bf16),
            jax.ShapeDtypeStruct((length, nq), bf16),
            jax.ShapeDtypeStruct((length // 2, D), bf16),
            jax.ShapeDtypeStruct((length // 2, D), f32),
        ],
        compiler_params=params(1),
        name="attend_forward",
    )(scal, a1, w_query, wkv, w_out, cosine, sine, marks, marks_t, *arrays)


def attend_backward(scal, dz, q, kdup, vdup, w_query, wkv, w_out, pieces, cosine, sine, marks, marks_t):
    length, D = dz.shape
    dh = w_query.shape[0]
    nq = w_query.shape[1] // 2
    pairs = nq // 128
    fw = dh // (lax.axis_size("dp") // 2)
    qkv_pieces = clip_pieces(pieces, 0, nq + 128)
    out_pieces = clip_pieces(pieces, nq + 128, 2 * nq + 128)
    arrays = unique_arrays(pieces)
    scale = HD ** (-0.5)
    rows = min(ROWS, length)

    def kernel(
        scal_ref, dz_ref, q_ref, kdup_ref, vdup_ref, wq_ref, wkv_ref, wo_ref,
        cos_ref, sin_ref, mk_ref, mt_ref, *rest
    ):
        piece_refs = rest[: len(arrays)]
        dq_ref, dkv_ref, send_ref, keep_ref = rest[len(arrays) : len(arrays) + 4]
        wq, woth, wo, wot, do, bias, dqs, dk, dv, sems = rest[len(arrays) + 4 :]
        e, k = scal_ref[0], scal_ref[1]
        step = pl.program_id(0)

        def first_copies():
            own = pltpu.make_async_copy(
                wo_ref.at[pl.ds(pl.multiple_of(k * nq, nq), nq), :], wo, sems.at[2]
            )
            return [own] + piece_copies(out_pieces, arrays, piece_refs, wot, e, fw, sems.at[3])

        def later_copies():
            own = pltpu.make_async_copy(
                wq_ref.at[:, pl.ds(pl.multiple_of(k * nq, nq), nq)], wq, sems.at[0]
            )
            return [own] + piece_copies(qkv_pieces, arrays, piece_refs, woth, e, fw, sems.at[1])

        @pl.when(step == 0)
        def _():
            copies = first_copies()
            start_all(copies)
            start_all(later_copies())
            same = mk_ref[:, 0:1] == mt_ref[0:1, :]
            before = mk_ref[:, 1:2] >= mt_ref[1:2, :]
            bias[...] = jnp.where(same & before, 0.0, masked_score)
            dk[...] = jnp.zeros_like(dk)
            dv[...] = jnp.zeros_like(dv)
            wait_all(copies)
            do[...] = (mm_t(dz_ref[:, :dh], wo[...]) + mm(dz_ref[:, dh:], wot[...])).astype(bf16)

        at = pl.ds(pl.multiple_of(step * 128, 128), 128)
        kd, vd = kdup_ref[...], vdup_ref[...]
        low = lanes_low((rows, 128))
        zero = jnp.zeros((rows, 128), bf16)
        for lo in range(0, length, rows):
            part = q_ref[lo : lo + rows, :]
            grad = do[lo : lo + rows, at]
            mask = bias[lo : lo + rows, :]
            outs = []
            for side in (0, 1):
                if side == 0:
                    qm, dom = jnp.where(low, part, zero), jnp.where(low, grad, zero)
                else:
                    qm, dom = jnp.where(low, zero, part), jnp.where(low, zero, grad)
                probs = softmax_rows(qm, kd, mask, scale)
                dprob = mm_t(dom, vd)
                centre = jnp.sum(probs * dprob, axis=1, keepdims=True)
                ds = (probs * (dprob - centre) * scale).astype(bf16)
                dv[...] += t_mm(probs.astype(bf16), dom)
                dk[...] += t_mm(ds, qm)
                outs.append(mm(ds, kd))
            value = jnp.where(low, outs[0], outs[1])
            value = turn(value, cos_ref[lo : lo + rows, :], -sin_ref[lo : lo + rows, :]).astype(bf16)
            dq_ref[lo : lo + rows, :] = value
            dqs[lo : lo + rows, at] = value

        @pl.when(step == pairs - 1)
        def _():
            dks = dk[...] + pltpu.roll(dk[...], HD, 1)
            dvs = dv[...] + pltpu.roll(dv[...], HD, 1)
            dks = turn(dks, cos_ref[...], -sin_ref[...])
            dkv = jnp.where(lanes_low(dks.shape), dks, dvs).astype(bf16)
            dkv_ref[...] = dkv
            wait_all(later_copies())
            dq_all = dqs[...]
            own = mm_t(dq_all, wq[...]) + mm_t(dkv, wkv_ref[...])
            split_store(own, send_ref, keep_ref, slice(0, dh))
            oth = mm_t(dq_all, woth[:, :nq]) + mm_t(dkv, woth[:, nq:])
            split_store(oth, send_ref, keep_ref, slice(dh, D))

    full = lambda shape: pl.BlockSpec(shape, lambda i, s: (0,) * len(shape))
    return pl.pallas_call(
        kernel,
        grid_spec=pltpu.PrefetchScalarGridSpec(
            num_scalar_prefetch=1,
            grid=(pairs,),
            in_specs=[
                full(dz.shape),
                pl.BlockSpec((length, 128), lambda i, s: (0, i)),
                full(kdup.shape),
                full(vdup.shape),
                ANY,
                full(wkv.shape),
                ANY,
            ]
            + [full(v.shape) for v in (cosine, sine, marks, marks_t)]
            + [ANY] * len(arrays),
            out_specs=[
                pl.BlockSpec((length, 128), lambda i, s: (0, i)),
                full((length, 128)),
                full((length // 2, D)),
                full((length // 2, D)),
            ],
            scratch_shapes=[
                pltpu.VMEM((dh, nq), bf16),
                pltpu.VMEM((dh, nq + 128), bf16),
                pltpu.VMEM((nq, dh), bf16),
                pltpu.VMEM((dh, nq), bf16),
                pltpu.VMEM((length, nq), bf16),
                pltpu.VMEM((length, length), f32),
                pltpu.VMEM((length, nq), bf16),
                pltpu.VMEM((length, 128), f32),
                pltpu.VMEM((length, 128), f32),
                pltpu.SemaphoreType.DMA((4,)),
            ],
        ),
        out_shape=[
            jax.ShapeDtypeStruct((length, nq), bf16),
            jax.ShapeDtypeStruct((length, 128), bf16),
            jax.ShapeDtypeStruct((length // 2, D), bf16),
            jax.ShapeDtypeStruct((length // 2, D), f32),
        ],
        compiler_params=params(1),
        name="attend_backward",
    )(scal, dz, q, kdup, vdup, w_query, wkv, w_out, cosine, sine, marks, marks_t, *arrays)


def tiles_of(n, width):
    return [(lo, min(n, lo + width)) for lo in range(0, n, width)]


def feed_middle(scal, a2, g, w_gate, w_up, w_down, pieces, lo, hi):
    length, D = a2.shape
    dh = w_gate.shape[0]
    hidden = w_gate.shape[1] // 2
    n = hi - lo
    fw = dh // (lax.axis_size("dp") // 2)
    arrays = unique_arrays(pieces)
    split = [clip_pieces(pieces, i * n, (i + 1) * n) for i in range(3)]

    def kernel(scal_ref, a_ref, g_ref, wg_ref, wu_ref, wd_ref, *rest):
        piece_refs = rest[: len(arrays)]
        m_ref, dgate_ref, dup_ref = rest[len(arrays) : len(arrays) + 3]
        wg, wu, wd, wdt, gate, up, sems = rest[len(arrays) + 3 :]
        e, k = scal_ref[0], scal_ref[1]
        start = pl.multiple_of(k * hidden + lo, 128)

        def copies(which):
            if which < 2:
                src, dst = ((wg_ref, wg), (wu_ref, wu))[which]
                own = pltpu.make_async_copy(
                    src.at[:, pl.ds(start, n)], dst.at[pl.ds(0, dh), :], sems.at[2 * which]
                )
                target = dst.at[pl.ds(dh, dh), :]
            else:
                own = pltpu.make_async_copy(wd_ref.at[pl.ds(start, n), :], wd, sems.at[4])
                target = wdt
            return [own] + piece_copies(
                split[which], arrays, piece_refs, target, e, fw, sems.at[2 * which + 1]
            )

        groups = [copies(i) for i in range(3)]
        for group in groups:
            start_all(group)
        wait_all(groups[0])
        for a, b in tiles_of(n, 256):
            gate[:, a:b] = mm(a_ref[...], wg[:, a:b])
        wait_all(groups[1])
        for a, b in tiles_of(n, 256):
            up[:, a:b] = mm(a_ref[...], wu[:, a:b])
        wait_all(groups[2])
        for a, b in tiles_of(n, 256):
            dm = mm_t(g_ref[:, :dh], wd[a:b, :]) + mm(g_ref[:, dh:], wdt[:, a:b])
            gt, ut = gate[:, a:b], up[:, a:b]
            sig = jax.nn.sigmoid(gt)
            act = gt * sig
            m_ref[:, a:b] = (act * ut).astype(bf16)
            dgate_ref[:, a:b] = (dm * ut * sig * (1.0 + gt * (1.0 - sig))).astype(bf16)
            dup_ref[:, a:b] = (dm * act).astype(bf16)

    full = lambda shape: pl.BlockSpec(shape, lambda i, s: (0,) * len(shape))
    return pl.pallas_call(
        kernel,
        grid_spec=pltpu.PrefetchScalarGridSpec(
            num_scalar_prefetch=1,
            grid=(1,),
            in_specs=[full(a2.shape), full(g.shape)] + [ANY] * (3 + len(arrays)),
            out_specs=[full((length, n))] * 3,
            scratch_shapes=[
                pltpu.VMEM((D, n), bf16),
                pltpu.VMEM((D, n), bf16),
                pltpu.VMEM((n, dh), bf16),
                pltpu.VMEM((dh, n), bf16),
                pltpu.VMEM((length, n), f32),
                pltpu.VMEM((length, n), f32),
                pltpu.SemaphoreType.DMA((6,)),
            ],
        ),
        out_shape=[jax.ShapeDtypeStruct((length, n), bf16)] * 3,
        compiler_params=params(1),
        name="feed_middle",
    )(scal, a2, g, w_gate, w_up, w_down, *arrays)


def feed_out(scal, kind, lefts, w_own, pieces, lo, hi, before, last):
    length = lefts[0].shape[0]
    n = hi - lo
    down = kind == "down"
    dh = w_own[0].shape[1] if down else w_own[0].shape[0]
    hidden = w_own[0].shape[0 if down else 1] // 2
    D = 2 * dh
    fw = dh // (lax.axis_size("dp") // 2)
    arrays = unique_arrays(pieces)
    ids = [2] if down else [0, 1]
    split = [clip_pieces(pieces, i * n, (i + 1) * n) for i in ids]
    extra = [] if before is None else [before]

    def kernel(scal_ref, *rest):
        left_refs, rest = rest[: len(lefts)], rest[len(lefts) :]
        own_refs, rest = rest[: len(lefts)], rest[len(lefts) :]
        piece_refs, rest = rest[: len(arrays)], rest[len(arrays) :]
        before_refs, rest = rest[: len(extra)], rest[len(extra) :]
        out_refs, rest = rest[: 2 if last else 1], rest[2 if last else 1 :]
        own_bufs, rest = rest[: len(lefts)], rest[len(lefts) :]
        oth_bufs, sems = rest[: len(lefts)], rest[len(lefts)]
        e, k = scal_ref[0], scal_ref[1]
        start = pl.multiple_of(k * hidden + lo, 128)
        own_copies, oth_copies = [], []
        for i in range(len(lefts)):
            src = own_refs[i]
            src = src.at[pl.ds(start, n), :] if down else src.at[:, pl.ds(start, n)]
            own_copies.append(pltpu.make_async_copy(src, own_bufs[i], sems.at[2 * i]))
            oth_copies += piece_copies(
                split[i], arrays, piece_refs, oth_bufs[i], e, fw, sems.at[2 * i + 1]
            )
        start_all(own_copies)
        start_all(oth_copies)

        def emit(value, a, b):
            if extra:
                value = value + before_refs[0][:, a:b]
            if last:
                split_store(value, out_refs[0], out_refs[1], slice(a, b))
            else:
                out_refs[0][:, a:b] = value

        wait_all(own_copies)
        for a, b in tiles_of(dh, 256):
            if down:
                value = mm(left_refs[0][...], own_bufs[0][:, a:b])
            else:
                value = mm_t(left_refs[0][...], own_bufs[0][a:b, :])
                value = value + mm_t(left_refs[1][...], own_bufs[1][a:b, :])
            emit(value, a, b)
        wait_all(oth_copies)
        for a, b in tiles_of(dh, 256):
            value = mm_t(left_refs[0][...], oth_bufs[0][a:b, :])
            if not down:
                value = value + mm_t(left_refs[1][...], oth_bufs[1][a:b, :])
            emit(value, dh + a, dh + b)

    full = lambda shape: pl.BlockSpec(shape, lambda i, s: (0,) * len(shape))
    half = (length // 2, D)
    if last:
        out_shape = [jax.ShapeDtypeStruct(half, bf16), jax.ShapeDtypeStruct(half, f32)]
    else:
        out_shape = [jax.ShapeDtypeStruct((length, D), f32)]
    own_shape = (n, dh) if down else (dh, n)
    out = pl.pallas_call(
        kernel,
        grid_spec=pltpu.PrefetchScalarGridSpec(
            num_scalar_prefetch=1,
            grid=(1,),
            in_specs=[full(v.shape) for v in lefts]
            + [ANY] * (len(lefts) + len(arrays))
            + [full(v.shape) for v in extra],
            out_specs=[full(v.shape) for v in out_shape],
            scratch_shapes=[pltpu.VMEM(own_shape, bf16)] * len(lefts)
            + [pltpu.VMEM((dh, n), bf16)] * len(lefts)
            + [pltpu.SemaphoreType.DMA((4,))],
        ),
        out_shape=out_shape,
        compiler_params=params(1),
        name="feed_" + kind,
    )(scal, *lefts, *w_own, *arrays, *extra)
    return out if last else out[0]


def grad_block(scal, j, groups, adds, first_cols):
    chips = lax.axis_size("dp") // 2
    length, D = groups[0][0].shape
    fw = D // 2 // chips
    rights = [v for _, vs in groups for v in vs]
    cols = sum(v.shape[1] for v in rights)

    def kernel(scal_ref, *rest):
        left_refs, rest = rest[: len(groups)], rest[len(groups) :]
        right_refs, rest = rest[: len(rights)], rest[len(rights) :]
        add_refs, outs = rest[: len(adds)], rest[len(adds) :]
        at, i = 0, 0
        for (_, vs), left_ref in zip(groups, left_refs):
            for v in vs:
                width = v.shape[1]
                value = t_mm(left_ref[...], right_refs[i][...])
                for (array, start), ref in zip(adds, add_refs):
                    a, b = max(at, start), min(at + width, start + array.shape[1])
                    if (a, b) == (at, at + width):
                        value = value + ref[:, a - start : b - start].astype(f32)
                    elif a < b:
                        parts = [value[:, a - at : b - at] + ref[:, a - start : b - start].astype(f32)]
                        if a > at:
                            parts = [value[:, : a - at]] + parts
                        if b < at + width:
                            parts = parts + [value[:, b - at :]]
                        value = jnp.concatenate(parts, 1)
                if j == 0:

                    @pl.when(pl.program_id(0) == 0)
                    def _(value=value, at=at, width=width):
                        outs[0][:, at : at + width] = value

                    @pl.when(pl.program_id(0) == 1)
                    def _(value=value, at=at, width=width):
                        outs[1][:, at : at + width] = value.astype(bf16)

                elif j == 3:
                    value = value.astype(bf16)
                    b = min(max(first_cols - at, 0), width)
                    if b > 0:
                        outs[0][:, at : at + b] = value[:, :b]
                    if b < width:
                        outs[1][:, at + b - first_cols : at + width - first_cols] = value[:, b:]
                else:
                    outs[0][:, at : at + width] = value.astype(bf16)
                at += width
                i += 1

    full = lambda shape: pl.BlockSpec(shape, lambda h, s: (0,) * len(shape))
    if j == 0:
        shapes = [((fw, cols), f32, full((fw, cols))), ((fw, cols), bf16, full((fw, cols)))]
    else:
        widths = (first_cols, cols - first_cols) if j == 3 else (cols,)
        shapes = [
            ((2 * fw, w), bf16, pl.BlockSpec((fw, w), lambda h, s: (h, 0))) for w in widths
        ]
    out = pl.pallas_call(
        kernel,
        grid_spec=pltpu.PrefetchScalarGridSpec(
            num_scalar_prefetch=1,
            grid=(2,),
            in_specs=[
                pl.BlockSpec((length, fw), lambda h, s: (0, h * chips + (s[0] ^ j)))
                for _ in groups
            ]
            + [full(v.shape) for v in rights]
            + [pl.BlockSpec((fw, v.shape[1]), lambda h, s: (h, 0)) for v, _ in adds],
            out_specs=[s[2] for s in shapes],
        ),
        out_shape=[jax.ShapeDtypeStruct(s[0], s[1]) for s in shapes],
        compiler_params=params(1),
        name=f"grad_block_{j}",
    )(scal, *[v for v, _ in groups], *rights, *[v for v, _ in adds])
    return out


def reduce_unit(scal, groups, first_cols):
    chips = lax.axis_size("dp") // 2
    if chips == 4:
        far_a, far_b = grad_block(scal, 3, groups, [], first_cols)
        got_a, got_b = swap_chip(far_a, 1), swap_chip(far_b, 0)
        got_x = swap_chip(grad_block(scal, 1, groups, [(got_a, 0)], first_cols)[0], 0)
        got_y = swap_chip(grad_block(scal, 2, groups, [(got_b, first_cols)], first_cols)[0], 1)
        own, oth = grad_block(scal, 0, groups, [(got_x, 0), (got_y, 0)], first_cols)
        return own + swap_row(oth).astype(f32)
    nbits = chips.bit_length() - 1
    e = scal[0]
    dh = groups[0][0].shape[1] // 2

    def make(keys):
        outs = []
        for left, rights in groups:
            left = jnp.concatenate(
                [xor_axis(left[:, :dh], e, 1, chips), xor_axis(left[:, dh:], e, 1, chips)], 1
            )
            left = take_keys(left, list(range(chips)), keys, 1)
            outs.append(t_mm(left, jnp.concatenate(rights, 1)))
        return jnp.concatenate(outs, 1)

    return reduce_features(make, list(range(nbits)), 0)


def tp_finish(send, keep):
    keep = keep + swap_core(send).astype(f32)
    half = keep.shape[0] // 2
    return keep[:half] + swap_col(keep[half:].astype(bf16)).astype(f32)


def on_device(
    tokens,
    segments,
    positions,
    attn_gain,
    w_query,
    w_key,
    w_value,
    w_out,
    mlp_gain,
    w_gate,
    w_up,
    w_down,
    cotangent,
):
    dp = lax.axis_index("dp")
    e, k = dp >> 1, dp & 1
    r, c = lax.axis_index("row"), lax.axis_index("col")
    chips = lax.axis_size("dp") // 2
    nbits = chips.bit_length() - 1
    scal = jnp.stack([e, k]).astype(jnp.int32)
    diag = k == r
    length = segments.shape[1]
    blk = length // 4
    dh = tokens.shape[2]
    D = 2 * dh
    fw = dh // chips
    nq = w_query.shape[1] // 2
    hidden = w_gate.shape[1] // 2
    first, second = side_perms()

    def spread_in(v):
        parts = v[0].reshape(2, blk, dh)
        here = jnp.where(r == 0, parts[0], parts[1])
        away = jnp.where(r == 0, parts[1], parts[0])
        got_a = permute_side(away, first)
        got_b = permute_side(here, second)
        own = jnp.where(diag, here, got_a)
        oth = jnp.where(diag, got_a, got_b)
        return jnp.concatenate([own, oth], 1)

    def spread_out(v):
        own, oth = v[:, :dh], v[:, dh:]
        got_a = permute_side(jnp.where(diag, oth, own), flip(first))
        got_b = permute_side(oth, flip(second))
        here = jnp.where(diag, own, got_b)
        return order_pair(here, got_a, r, 0)[None]

    gains = jnp.stack([attn_gain, mlp_gain])
    gains = jnp.concatenate([gains, swap_row(gains)], 1)
    meta = jnp.concatenate([segments, positions], 0)
    meta = jnp.where(diag, meta, swap_core(meta))
    place = jnp.arange(length, dtype=jnp.int32)[None]
    meta = jnp.concatenate([meta, place], 0)
    quarter = jnp.split(meta, 4, 1)
    meta = jnp.concatenate(
        xor_blocks([quarter[0], quarter[2], quarter[1], quarter[3]], 2 * k + c), 1
    )
    marks_t = jnp.stack([meta[0], meta[2]])
    marks = marks_t.T
    half = HD // 2
    frequency = 10000.0 ** (-jnp.arange(half, dtype=f32) * 2.0 / HD)
    angles = meta[1].astype(f32)[:, None] * frequency[None, :]
    cosine, sine = jnp.cos(angles), jnp.sin(angles)
    cosine = jnp.concatenate([cosine] * 4, 1)
    sine = jnp.concatenate([-sine, sine] * 2, 1)

    x = spread_in(tokens)
    wkv = jnp.concatenate([pick(w_key, k, 1), pick(w_value, k, 1)], 1)

    def rows_shard(w, start, size):
        return lax.dynamic_slice(w, (e * fw, start), (fw, size))

    def cols_shard(w, start, size):
        return lax.dynamic_slice(w, (start, e * fw), (size, fw)).T

    shard = jnp.concatenate(
        [
            rows_shard(w_query, k * nq, nq),
            rows_shard(wkv, 0, 128),
            cols_shard(w_out, k * nq, nq),
        ],
        1,
    )
    attn_pieces = gather_unit(swap_row(shard), 640)
    g = spread_in(cotangent)
    unit = 128
    spans = [(0, 640), (640, hidden)]
    feed_pieces = []
    for lo, hi in spans:
        n = hi - lo
        at = k * hidden + lo
        shard = jnp.concatenate(
            [rows_shard(w_gate, at, n), rows_shard(w_up, at, n), cols_shard(w_down, at, n)], 1
        )
        feed_pieces.append(gather_unit(swap_row(shard), 3 * n // 256 * 128))

    xf = x.astype(f32)
    r1 = lax.rsqrt(jnp.sum(xf * xf, axis=1, keepdims=True) / D + epsilon)
    a1 = tp_gather((xf * r1 * gains[0]).astype(bf16))
    q, kdup, vdup, o, send, keep = attend_forward(
        scal, a1, w_query, wkv, w_out, attn_pieces, cosine, sine, marks, marks_t
    )
    hres = xf + tp_finish(send, keep)
    r2 = lax.rsqrt(jnp.sum(hres * hres, axis=1, keepdims=True) / D + epsilon)
    a2 = tp_gather((hres * r2 * gains[1]).astype(bf16))
    g_all = tp_gather(g)

    out_part, da2_part = None, None
    feed_sums = []
    for i, ((lo, hi), pieces) in enumerate(zip(spans, feed_pieces)):
        last = i == len(spans) - 1
        m, dgate, dup = feed_middle(scal, a2, g_all, w_gate, w_up, w_down, pieces, lo, hi)
        da2_part = feed_out(
            scal, "in", [dgate, dup], [w_gate, w_up], pieces, lo, hi, da2_part, last
        )
        n = hi - lo
        feed_sums.append(
            reduce_unit(scal, [(a2, [dgate, dup]), (g_all, [m])], 3 * n // 256 * 128)
        )
        out_part = feed_out(scal, "down", [m], [w_down], pieces, lo, hi, out_part, last)
    result = spread_out((hres + tp_finish(*out_part)).astype(bf16))

    def norm_back(inputs, factor, gain, upstream):
        weighted = upstream * gain
        dotted = jnp.sum(weighted * inputs, axis=1, keepdims=True)
        grad = factor * weighted - inputs * factor**3 * dotted / D
        return grad, jnp.sum(upstream * inputs * factor, axis=0)

    dh_grad, gain_two = norm_back(hres, r2, gains[1], tp_finish(*da2_part))
    dh_grad = dh_grad + g.astype(f32)
    dz = tp_gather(dh_grad.astype(bf16))
    dq, dkv, send, keep = attend_backward(
        scal, dz, q, kdup, vdup, w_query, wkv, w_out, attn_pieces, cosine, sine, marks, marks_t
    )
    out_sum = reduce_unit(scal, [(dz, [o])], 256)
    qkv_sum = reduce_unit(scal, [(a1, [dq, dkv])], 256)
    grad_x, gain_one = norm_back(xf, r1, gains[0], tp_finish(send, keep))
    grad_x = spread_out((grad_x + dh_grad).astype(bf16))

    both = jnp.stack([gain_one, gain_two])
    own = both[:, :dh] + swap_row(both[:, dh:])
    own = own + swap_col(own)
    own = own + swap_core(own)
    for bit in range(nbits):
        own = own + swap_chip(own, bit)

    def rows_home(v):
        return pick(v, k, 0), swap_core(pick(v, 1 - k, 0))

    homes = []
    for (lo, hi), v in zip(spans, feed_sums):
        homes.append(rows_home(v[:, : 2 * (hi - lo)]))
    grads = []
    for which in range(2):
        sides = []
        for side in range(2):
            for (lo, hi), home in zip(spans, homes):
                n = hi - lo
                sides.append(home[side][:, which * n : (which + 1) * n])
        mine = jnp.concatenate(sides[: len(spans)], 1)
        theirs = jnp.concatenate(sides[len(spans) :], 1)
        grads.append(order_pair(mine, theirs, k, 1))
    grad_gate, grad_up = grads
    mine, theirs = rows_home(qkv_sum)
    grad_query = order_pair(mine[:, :nq], theirs[:, :nq], k, 1)
    grad_key = order_pair(mine[:, nq : nq + HD], theirs[:, nq : nq + HD], k, 1)
    grad_value = order_pair(mine[:, nq + HD :], theirs[:, nq + HD :], k, 1)

    def exchange(v):
        v = v.astype(bf16).T
        rows = v.shape[0] // chips
        view = v.reshape(chips // 2, 2, rows, v.shape[1])
        mine = jnp.where(k == 0, view[:, 0], view[:, 1])
        got = swap_core(jnp.where(k == 0, view[:, 1], view[:, 0]))
        full = order_pair(mine, got, k, 0)
        rel = xor_blocks([full[i] for i in range(chips)], e)
        n = lax.axis_size("dp")
        out = [rel[0]]
        for j in range(1, chips):
            out.append(lax.ppermute(rel[j], "dp", [(i, i ^ (2 * j)) for i in range(n)]))
        return jnp.concatenate(xor_blocks(out, e), 1).astype(f32)

    downs = [v[:, 2 * (hi - lo) :] for (lo, hi), v in zip(spans, feed_sums)]
    grad_down = exchange(jnp.concatenate(downs, 1))
    grad_out = exchange(out_sum)
    return (
        result,
        grad_x,
        own[0],
        grad_query[None],
        grad_key[None],
        grad_value[None],
        grad_out[None],
        own[1],
        grad_gate[None],
        grad_up[None],
        grad_down[None],
    )


def solution(mesh):
    placed = (
        P("dp", "col", "row"),
        P("dp", None),
        P("dp", None),
        P("row"),
        P("row", "col"),
        P("row", "col"),
        P("row", "col"),
        P("col", "row"),
        P("row"),
        P("row", "col"),
        P("row", "col"),
        P("col", "row"),
        P("dp", "col", "row"),
    )
    return jax.shard_map(
        on_device,
        mesh=mesh,
        in_specs=placed,
        out_specs=(
            P("dp", "col", "row"),
            P("dp", "col", "row"),
            P("row"),
            P("row", "dp", "col"),
            P("row", "dp", "col"),
            P("row", "dp", "col"),
            P("col", "dp", "row"),
            P("row"),
            P("row", "dp", "col"),
            P("row", "dp", "col"),
            P("col", "dp", "row"),
        ),
        check_vma=False,
    )
```

```python
import jax
import jax.numpy as jnp
from jax import lax
from jax.experimental import pallas as pl
from jax.experimental.pallas import tpu as pltpu
from jax.sharding import PartitionSpec as P


HD = 64
epsilon = 1e-05
masked_score = -1e30
f32 = jnp.float32
bf16 = jnp.bfloat16


def swap_core(v):
    n = lax.axis_size("dp")
    return lax.ppermute(v, "dp", [(i, i ^ 1) for i in range(n)])


def swap_chip(v, bit):
    n = lax.axis_size("dp")
    return lax.ppermute(v, "dp", [(i, i ^ (2 << bit)) for i in range(n)])


def swap_row(v):
    return lax.ppermute(v, "row", [(0, 1), (1, 0)])


def swap_col(v):
    return lax.ppermute(v, "col", [(0, 1), (1, 0)])


def side_perms():
    chips = lax.axis_size("dp") // 2
    first, second = [], []
    for e in range(chips):
        for a in range(2):
            same = (2 * e + a) * 2 + a
            other = (2 * e + a) * 2 + 1 - a
            mate = (2 * e + 1 - a) * 2 + a
            first += [(same, mate), (other, same)]
            second += [(other, mate)]
    return first, second


def flip(perm):
    return [(b, a) for a, b in perm]


def xor_blocks(blocks, index):
    bit = 0
    while (1 << bit) < len(blocks):
        on = ((index >> bit) & 1) == 1
        blocks = [jnp.where(on, blocks[i ^ (1 << bit)], blocks[i]) for i in range(len(blocks))]
        bit += 1
    return blocks


def xor_axis(v, index, axis, count):
    return jnp.concatenate(xor_blocks(jnp.split(v, count, axis), index), axis)


def pick(v, index, axis):
    lo, hi = jnp.split(v, 2, axis)
    return jnp.where(index == 0, lo, hi)


def order_pair(mine, theirs, index, axis):
    return jnp.where(
        index == 0,
        jnp.concatenate([mine, theirs], axis),
        jnp.concatenate([theirs, mine], axis),
    )


def mm(a, b):
    return jnp.dot(a, b, preferred_element_type=f32)


def mm_t(a, b):
    return lax.dot_general(a, b, (((1,), (1,)), ((), ())), preferred_element_type=f32)


def t_mm(a, b):
    return lax.dot_general(a, b, (((0,), (0,)), ((), ())), preferred_element_type=f32)


def tp_gather(v):
    mate = swap_col(v)
    return [v, mate, swap_core(v), swap_core(mate)]


def gather_chips(shard, bits, axis):
    held = {0: shard}
    for bit in bits:
        keys = list(held)
        got = swap_chip(jnp.concatenate([held[j] for j in keys], axis), bit)
        for j, piece in zip(keys, jnp.split(got, len(keys), axis)):
            held[j ^ (1 << bit)] = piece
    return jnp.concatenate([held[j] for j in range(len(held))], axis)


def cut(v, start, size, axis):
    return lax.slice_in_dim(v, start, start + size, axis=axis)


def take_keys(v, have, want, axis):
    width = v.shape[axis] // (2 * len(have))
    out = []
    for h in range(2):
        for j in want:
            out.append(cut(v, (h * len(have) + have.index(j)) * width, width, axis))
    return out[0] if len(out) == 1 else jnp.concatenate(out, axis)


def reduce_features(make, bits, axis):
    count = 1 << len(bits)
    keys = list(range(count))
    got = []

    def total(want):
        value = make(want)
        for have, arr in got:
            value = value + take_keys(arr, have, want, axis).astype(f32)
        return value

    for bit in bits:
        send = [j for j in keys if (j >> bit) & 1]
        keys = [j for j in keys if not (j >> bit) & 1]
        arr = swap_chip(total(send).astype(bf16), bit)
        got.append(([j ^ (1 << bit) for j in send], arr))
    own, other = jnp.split(total(keys), 2, axis)
    return own + swap_row(other.astype(bf16)).astype(f32)


ANY = pl.BlockSpec(memory_space=pl.ANY)
LIMIT = 60 << 20
TILE = 256
WIDE = 512


def params(dims):
    return pltpu.CompilerParams(
        dimension_semantics=("arbitrary",) * dims, vmem_limit_bytes=LIMIT
    )


def gather_unit(shard, first_cols, at=0):
    chips = lax.axis_size("dp") // 2
    rows, cols = shard.shape
    if chips == 4:
        got_x, got_y = swap_chip(shard, 0), swap_chip(shard, 1)
        far_a = swap_chip(got_x[:, :first_cols], 1)
        far_b = swap_chip(got_y[:, first_cols:], 0)
        return [
            (shard, 0, 0, 0, cols, at),
            (got_x, 0, 1, 0, cols, at),
            (got_y, 0, 2, 0, cols, at),
            (far_a, 0, 3, 0, first_cols, at),
            (far_b, 0, 3, 0, cols - first_cols, at + first_cols),
        ]
    nbits = chips.bit_length() - 1
    whole = gather_chips(shard, list(range(nbits)), 0)
    return [(whole, j * rows, j, 0, cols, at) for j in range(chips)]


def clip_pieces(pieces, lo, hi):
    out = []
    for array, row, j, col, count, at in pieces:
        a, b = max(lo, at), min(hi, at + count)
        if a < b:
            out.append((array, row, j, col + a - at, b - a, a - lo))
    return out


def unique_arrays(pieces):
    arrays = []
    for piece in pieces:
        if not any(piece[0] is a for a in arrays):
            arrays.append(piece[0])
    return arrays


def piece_copies(pieces, arrays, refs, target, e, fw, sem):
    copies = []
    for array, row, j, col, count, at in pieces:
        ref = refs[[a is array for a in arrays].index(True)]
        copies.append(
            pltpu.make_async_copy(
                ref.at[pl.ds(row, fw), pl.ds(col, count)],
                target.at[pl.ds(pl.multiple_of((e ^ j) * fw, fw), fw), pl.ds(at, count)],
                sem,
            )
        )
    return copies


def start_all(copies):
    for copy in copies:
        copy.start()


def wait_all(copies):
    for copy in copies:
        copy.wait()


def lanes_low(shape):
    return lax.broadcasted_iota(jnp.int32, shape, 1) % 128 < HD


def turn(x, cosine, sine):
    lane = lax.broadcasted_iota(jnp.int32, x.shape, 1) % HD
    mate = jnp.where(lane < HD // 2, pltpu.roll(x, 128 - HD // 2, 1), pltpu.roll(x, HD // 2, 1))
    return x * cosine + mate * sine


def place_of(scal_ref, i, blk):
    k, c = scal_ref[1], scal_ref[2]
    local = ((i & 1) ^ k) * 2 + ((i >> 1) ^ c)
    return pl.ds(pl.multiple_of(local * blk, blk), blk)


def fill_bias(bias, mk_ref, mt_ref):
    shape = bias.shape
    before = lax.broadcasted_iota(jnp.int32, shape, 0) >= lax.broadcasted_iota(jnp.int32, shape, 1)
    bias[...] = jnp.where((mk_ref[...] == mt_ref[...]) & before, 0.0, masked_score)


def two_heads(x):
    low = lanes_low(x.shape)
    zero = jnp.zeros(x.shape, x.dtype)
    return jnp.concatenate([jnp.where(low, x, zero), jnp.where(low, zero, x)], 0)


def one_row(x):
    rows = x.shape[0] // 2
    return jnp.where(lanes_low((rows, x.shape[1])), x[:rows], x[rows:])


def softmax_rows(qm, kdup, bias, scale):
    scores = mm_t(qm, kdup) * scale + jnp.concatenate([bias, bias], 0)
    top = jnp.max(scores, axis=1, keepdims=True)
    weights = jnp.exp(scores - top)
    return weights * (1.0 / jnp.sum(weights, axis=1, keepdims=True))


def split_store(value, send_ref, keep_ref, cols):
    half = value.shape[0] // 2
    keep_ref[:, cols] = value[:half]
    send_ref[:, cols] = value[half:].astype(bf16)


def attend_forward(scal, a_src, w_query, wkv, w_out, pieces, cosine, sine, marks, marks_t):
    length, D = segments_length(a_src), a_src[0].shape[1]
    dh = w_query.shape[0]
    nq = w_query.shape[1] // 2
    pairs = nq // 128
    fw = dh // (lax.axis_size("dp") // 2)
    qkv_pieces = clip_pieces(pieces, 0, nq + 128)
    out_pieces = clip_pieces(pieces, nq + 128, 2 * nq + 128)
    arrays = unique_arrays(pieces)
    scale = HD ** (-0.5)
    blk = length // 4

    def kernel(scal_ref, *rest):
        a_refs, rest = rest[: len(a_src)], rest[len(a_src) :]
        (wq_ref, wkv_ref, wo_ref, cos_ref, sin_ref, mk_ref, mt_ref), rest = rest[:7], rest[7:]
        piece_refs = rest[: len(arrays)]
        q_ref, kdup_ref, vdup_ref, o_ref, send_ref, keep_ref, a_out = rest[len(arrays) : len(arrays) + 7]
        a_ref, wq, woth, wo, wot, qkv, kloc, vloc, bias, attended, sems = rest[len(arrays) + 7 :]
        e, k = scal_ref[0], scal_ref[1]
        step = pl.program_id(0)

        def first_copies():
            own = pltpu.make_async_copy(
                wq_ref.at[:, pl.ds(pl.multiple_of(k * nq, nq), nq)], wq, sems.at[0]
            )
            return [own] + piece_copies(qkv_pieces, arrays, piece_refs, woth, e, fw, sems.at[1])

        def later_copies():
            own = pltpu.make_async_copy(
                wo_ref.at[pl.ds(pl.multiple_of(k * nq, nq), nq), :], wo, sems.at[2]
            )
            return [own] + piece_copies(out_pieces, arrays, piece_refs, wot, e, fw, sems.at[3])

        @pl.when(step == 0)
        def _():
            copies = gather_tokens(a_refs, a_ref, sems.at[4]) + first_copies()
            start_all(copies)
            start_all(later_copies())
            fill_bias(bias, mk_ref, mt_ref)
            wait_all(copies)
            pltpu.make_async_copy(a_ref, a_out, sems.at[5]).start()
            a_own, a_oth = a_ref[:, :dh], a_ref[:, dh:]
            qkv[:, :nq] = mm(a_own, wq[...]) + mm(a_oth, woth[:, :nq])
            kv = mm(a_own, wkv_ref[...]) + mm(a_oth, woth[:, nq:])
            low = lanes_low(kv.shape)
            kv = jnp.where(low, turn(kv, cos_ref[...], sin_ref[...]), kv)
            swapped = pltpu.roll(kv, HD, 1)
            kloc[...] = jnp.where(low, kv, swapped)
            vloc[...] = jnp.where(low, swapped, kv)
            for i in range(4):
                rows = place_of(scal_ref, i, blk)
                kdup_ref[i * blk : (i + 1) * blk, :] = kloc[rows, :].astype(bf16)
                vdup_ref[i * blk : (i + 1) * blk, :] = vloc[rows, :].astype(bf16)

        at = pl.ds(pl.multiple_of(step * 128, 128), 128)
        q = turn(qkv[:, at], cos_ref[...], sin_ref[...]).astype(bf16)
        q_ref[...] = q
        for i in range(4):
            rows = place_of(scal_ref, i, blk)
            keys = (i + 1) * blk
            mask = bias[i * blk : keys, :keys]
            probs = softmax_rows(two_heads(q_ref[rows, :]), kdup_ref[:keys, :], mask, scale)
            value = one_row(mm(probs.astype(bf16), vdup_ref[:keys, :])).astype(bf16)
            o_ref[rows, :] = value
            attended[rows, at] = value

        @pl.when(step == pairs - 1)
        def _():
            wait_all(later_copies() + [pltpu.make_async_copy(a_ref, a_out, sems.at[5])])
            o = attended[...]
            split_store(mm(o, wo[...]), send_ref, keep_ref, slice(0, dh))
            split_store(mm_t(o, wot[...]), send_ref, keep_ref, slice(dh, D))

    full = lambda shape: pl.BlockSpec(shape, lambda i, s: (0,) * len(shape))
    return pl.pallas_call(
        kernel,
        grid_spec=pltpu.PrefetchScalarGridSpec(
            num_scalar_prefetch=1,
            grid=(pairs,),
            in_specs=[ANY] * len(a_src)
            + [ANY, full(wkv.shape), ANY]
            + [full(v.shape) for v in (cosine, sine, marks, marks_t)]
            + [ANY] * len(arrays),
            out_specs=[
                pl.BlockSpec((length, 128), lambda i, s: (0, i)),
                full((length, 128)),
                full((length, 128)),
                pl.BlockSpec((length, 128), lambda i, s: (0, i)),
                full((length // 2, D)),
                full((length // 2, D)),
                ANY,
            ],
            scratch_shapes=[
                pltpu.VMEM((length, D), bf16),
                pltpu.VMEM((dh, nq), bf16),
                pltpu.VMEM((dh, nq + 128), bf16),
                pltpu.VMEM((nq, dh), bf16),
                pltpu.VMEM((dh, nq), bf16),
                pltpu.VMEM((length, nq), f32),
                pltpu.VMEM((length, 128), f32),
                pltpu.VMEM((length, 128), f32),
                pltpu.VMEM((length, length), f32),
                pltpu.VMEM((length, nq), bf16),
                pltpu.SemaphoreType.DMA((6,)),
            ],
        ),
        out_shape=[
            jax.ShapeDtypeStruct((length, nq), bf16),
            jax.ShapeDtypeStruct((length, 128), bf16),
            jax.ShapeDtypeStruct((length, 128), bf16),
            jax.ShapeDtypeStruct((length, nq), bf16),
            jax.ShapeDtypeStruct((length // 2, D), bf16),
            jax.ShapeDtypeStruct((length // 2, D), f32),
            jax.ShapeDtypeStruct((length, D), bf16),
        ],
        compiler_params=params(1),
        name="attend_forward",
    )(scal, *a_src, w_query, wkv, w_out, cosine, sine, marks, marks_t, *arrays)


def attend_backward(scal, z_src, q, kdup, vdup, w_query, wkv, w_out, pieces, cosine, sine, marks, marks_t):
    length, D = segments_length(z_src), z_src[0].shape[1]
    dh = w_query.shape[0]
    nq = w_query.shape[1] // 2
    pairs = nq // 128
    fw = dh // (lax.axis_size("dp") // 2)
    qkv_pieces = clip_pieces(pieces, 0, nq + 128)
    out_pieces = clip_pieces(pieces, nq + 128, 2 * nq + 128)
    arrays = unique_arrays(pieces)
    scale = HD ** (-0.5)
    blk = length // 4

    def kernel(scal_ref, *rest):
        z_refs, rest = rest[: len(z_src)], rest[len(z_src) :]
        q_ref, kdup_ref, vdup_ref, wq_ref, wkv_ref, wo_ref = rest[:6]
        (cos_ref, sin_ref, mk_ref, mt_ref), rest = rest[6:10], rest[10:]
        piece_refs = rest[: len(arrays)]
        dq_ref, dkv_ref, send_ref, keep_ref, z_out = rest[len(arrays) : len(arrays) + 5]
        dz_ref, wq, woth, wo, wot, do, bias, dqs, dk, dv, sems = rest[len(arrays) + 5 :]
        e, k = scal_ref[0], scal_ref[1]
        step = pl.program_id(0)

        def first_copies():
            own = pltpu.make_async_copy(
                wo_ref.at[pl.ds(pl.multiple_of(k * nq, nq), nq), :], wo, sems.at[2]
            )
            return [own] + piece_copies(out_pieces, arrays, piece_refs, wot, e, fw, sems.at[3])

        def later_copies():
            own = pltpu.make_async_copy(
                wq_ref.at[:, pl.ds(pl.multiple_of(k * nq, nq), nq)], wq, sems.at[0]
            )
            return [own] + piece_copies(qkv_pieces, arrays, piece_refs, woth, e, fw, sems.at[1])

        @pl.when(step == 0)
        def _():
            copies = gather_tokens(z_refs, dz_ref, sems.at[4]) + first_copies()
            start_all(copies)
            start_all(later_copies())
            fill_bias(bias, mk_ref, mt_ref)
            dk[...] = jnp.zeros_like(dk)
            dv[...] = jnp.zeros_like(dv)
            wait_all(copies)
            pltpu.make_async_copy(dz_ref, z_out, sems.at[5]).start()
            do[...] = (mm_t(dz_ref[:, :dh], wo[...]) + mm(dz_ref[:, dh:], wot[...])).astype(bf16)

        at = pl.ds(pl.multiple_of(step * 128, 128), 128)
        for i in range(4):
            rows = place_of(scal_ref, i, blk)
            keys = (i + 1) * blk
            mask = bias[i * blk : keys, :keys]
            kd, vd = kdup_ref[:keys, :], vdup_ref[:keys, :]
            qm, dom = two_heads(q_ref[rows, :]), two_heads(do[rows, at])
            probs = softmax_rows(qm, kd, mask, scale)
            dprob = mm_t(dom, vd)
            centre = jnp.sum(probs * dprob, axis=1, keepdims=True)
            ds = (probs * (dprob - centre) * scale).astype(bf16)
            dv[:keys, :] += t_mm(probs.astype(bf16), dom)
            dk[:keys, :] += t_mm(ds, qm)
            value = turn(one_row(mm(ds, kd)), cos_ref[rows, :], -sin_ref[rows, :]).astype(bf16)
            dq_ref[rows, :] = value
            dqs[rows, at] = value

        @pl.when(step == pairs - 1)
        def _():
            for i in range(4):
                rows = place_of(scal_ref, i, blk)
                part = slice(i * blk, (i + 1) * blk)
                dks = dk[part, :] + pltpu.roll(dk[part, :], HD, 1)
                dvs = dv[part, :] + pltpu.roll(dv[part, :], HD, 1)
                dks = turn(dks, cos_ref[rows, :], -sin_ref[rows, :])
                dkv_ref[rows, :] = jnp.where(lanes_low(dks.shape), dks, dvs).astype(bf16)
            dkv = dkv_ref[...]
            wait_all(later_copies() + [pltpu.make_async_copy(dz_ref, z_out, sems.at[5])])
            dq_all = dqs[...]
            own = mm_t(dq_all, wq[...]) + mm_t(dkv, wkv_ref[...])
            split_store(own, send_ref, keep_ref, slice(0, dh))
            oth = mm_t(dq_all, woth[:, :nq]) + mm_t(dkv, woth[:, nq:])
            split_store(oth, send_ref, keep_ref, slice(dh, D))

    full = lambda shape: pl.BlockSpec(shape, lambda i, s: (0,) * len(shape))
    return pl.pallas_call(
        kernel,
        grid_spec=pltpu.PrefetchScalarGridSpec(
            num_scalar_prefetch=1,
            grid=(pairs,),
            in_specs=[ANY] * len(z_src)
            + [
                pl.BlockSpec((length, 128), lambda i, s: (0, i)),
                full(kdup.shape),
                full(vdup.shape),
                ANY,
                full(wkv.shape),
                ANY,
            ]
            + [full(v.shape) for v in (cosine, sine, marks, marks_t)]
            + [ANY] * len(arrays),
            out_specs=[
                pl.BlockSpec((length, 128), lambda i, s: (0, i)),
                full((length, 128)),
                full((length // 2, D)),
                full((length // 2, D)),
                ANY,
            ],
            scratch_shapes=[
                pltpu.VMEM((length, D), bf16),
                pltpu.VMEM((dh, nq), bf16),
                pltpu.VMEM((dh, nq + 128), bf16),
                pltpu.VMEM((nq, dh), bf16),
                pltpu.VMEM((dh, nq), bf16),
                pltpu.VMEM((length, nq), bf16),
                pltpu.VMEM((length, length), f32),
                pltpu.VMEM((length, nq), bf16),
                pltpu.VMEM((length, 128), f32),
                pltpu.VMEM((length, 128), f32),
                pltpu.SemaphoreType.DMA((6,)),
            ],
        ),
        out_shape=[
            jax.ShapeDtypeStruct((length, nq), bf16),
            jax.ShapeDtypeStruct((length, 128), bf16),
            jax.ShapeDtypeStruct((length // 2, D), bf16),
            jax.ShapeDtypeStruct((length // 2, D), f32),
            jax.ShapeDtypeStruct((length, D), bf16),
        ],
        compiler_params=params(1),
        name="attend_backward",
    )(scal, *z_src, q, kdup, vdup, w_query, wkv, w_out, cosine, sine, marks, marks_t, *arrays)


def each_tile(n, width, body, unroll=False):
    if unroll or n % width:
        for lo in range(0, n, width):
            body(slice(lo, min(n, lo + width)), lo)
        return

    def step(i, carry):
        start = pl.multiple_of(i * width, width)
        body(pl.ds(start, width), start)
        return carry

    lax.fori_loop(0, n // width, step, 0)


def gather_tokens(sources, target, sem):
    if len(sources) == 1:
        return [pltpu.make_async_copy(sources[0], target, sem)]
    blk = target.shape[0] // len(sources)
    return [
        pltpu.make_async_copy(source, target.at[pl.ds(i * blk, blk), :], sem)
        for i, source in enumerate(sources)
    ]


def leave_block(buf, j, first_cols, outs, sems, base):
    far_a, far_b, b1a, b2b, b0 = outs
    rows, cols = buf.shape[1], buf.shape[2]
    left = buf.at[j, :, pl.ds(0, first_cols)]
    right = buf.at[j, :, pl.ds(first_cols, cols - first_cols)]
    copy = pltpu.make_async_copy
    if j == 3:
        return [
            copy(left, far_a.at[pl.ds(0, rows), :], sems.at[base]),
            copy(right, far_b.at[pl.ds(0, rows), :], sems.at[base + 1]),
        ]
    if j == 2:
        return [
            copy(left, far_a.at[pl.ds(rows, rows), :], sems.at[base + 2]),
            copy(right, b2b, sems.at[base + 3]),
        ]
    if j == 1:
        return [
            copy(left, b1a, sems.at[base + 4]),
            copy(right, far_b.at[pl.ds(rows, rows), :], sems.at[base + 5]),
        ]
    return [copy(buf.at[0], b0, sems.at[base + 6])]


def block_shapes(fw, cols, first_cols):
    rest = cols - first_cols
    sizes = [(4 * fw, first_cols), (4 * fw, rest), (2 * fw, first_cols), (2 * fw, rest), (2 * fw, cols)]
    return [jax.ShapeDtypeStruct(size, bf16) for size in sizes]


def feed_first(scal, a_src, g_src, w_gate, w_up, w_down, pieces, lo, hi, first_cols):
    length, D = segments_length(a_src), a_src[0].shape[1]
    dh = w_gate.shape[0]
    chips = lax.axis_size("dp") // 2
    hidden = w_gate.shape[1] // 2
    n = hi - lo
    fw = dh // chips
    arrays = unique_arrays(pieces)
    split = [clip_pieces(pieces, i * n, (i + 1) * n) for i in range(3)]
    blocks = chips == 4
    whole = len(a_src) > 1
    cols = 3 * n

    def kernel(scal_ref, *rest):
        a_refs, rest = rest[: len(a_src)], rest[len(a_src) :]
        g_refs, rest = rest[: len(g_src)], rest[len(g_src) :]
        wg_ref, wu_ref, wd_ref = rest[:3]
        piece_refs, rest = rest[3 : 3 + len(arrays)], rest[3 + len(arrays) :]
        d_ref, rest = rest[0], rest[1:]
        if blocks:
            far_a, far_b, b1a, b2b, b0 = rest[:5]
            rest = rest[5:]
        if whole:
            a_out, g_out = rest[:2]
            rest = rest[2:]
        a_buf, g_buf, wg, wu, wd, wdt, gate, up, buf, sems = rest
        e, k = scal_ref[0], scal_ref[1]
        start = pl.multiple_of(k * hidden + lo, 128)

        def copies(which):
            if which < 2:
                src, dst = ((wg_ref, wg), (wu_ref, wu))[which]
                own = pltpu.make_async_copy(
                    src.at[:, pl.ds(start, n)], dst.at[pl.ds(0, dh), :], sems.at[2 * which]
                )
                target = dst.at[pl.ds(dh, dh), :]
            else:
                own = pltpu.make_async_copy(wd_ref.at[pl.ds(start, n), :], wd, sems.at[4])
                target = wdt
            return [own] + piece_copies(
                split[which], arrays, piece_refs, target, e, fw, sems.at[2 * which + 1]
            )

        a_in = gather_tokens(a_refs, a_buf, sems.at[6])
        g_in = gather_tokens(g_refs, g_buf, sems.at[7])
        groups = [copies(i) for i in range(3)]
        start_all(a_in)
        start_all(groups[0])
        start_all(groups[1])
        start_all(g_in)
        start_all(groups[2])
        wait_all(a_in)
        wait_all(groups[0])

        def gates(at, start):
            gate[:, at] = mm(a_buf[...], wg[:, at])

        def ups(at, start):
            up[:, at] = mm(a_buf[...], wu[:, at])

        def middle(at, start):
            dm = mm_t(g_buf[:, :dh], wd[at, :]) + mm(g_buf[:, dh:], wdt[:, at])
            gt, ut = gate[:, at], up[:, at]
            sig = jax.nn.sigmoid(gt)
            act = gt * sig
            width = dm.shape[1]
            d_ref[:, at] = (dm * ut * sig * (1.0 + gt * (1.0 - sig))).astype(bf16)
            d_ref[:, pl.ds(n + start, width)] = (dm * act).astype(bf16)
            d_ref[:, pl.ds(2 * n + start, width)] = (act * ut).astype(bf16)

        each_tile(n, TILE, gates, True)
        wait_all(groups[1])
        each_tile(n, TILE, ups, True)
        wait_all(g_in)
        wait_all(groups[2])
        each_tile(n, TILE, middle, True)
        outs = []
        if whole:
            outs += [
                pltpu.make_async_copy(a_buf, a_out, sems.at[8]),
                pltpu.make_async_copy(g_buf, g_out, sems.at[9]),
            ]
            start_all(outs)
        if blocks:

            def leave(j):
                return leave_block(buf, j, first_cols, (far_a, far_b, b1a, b2b, b0), sems, 10)

            def one(i, carry):
                j, h = 3 - i // 2, i % 2
                at = pl.ds(pl.multiple_of(h * dh + (e ^ j) * fw, fw), fw)
                rows = pl.ds(pl.multiple_of(h * fw, fw), fw)
                left = a_buf[:, at]
                buf[j, rows, : 2 * n] = t_mm(left, d_ref[:, : 2 * n]).astype(bf16)
                buf[j, rows, 2 * n :] = t_mm(g_buf[:, at], d_ref[:, 2 * n :]).astype(bf16)
                for jj in range(4):

                    @pl.when((j == jj) & (h == 1))
                    def _(jj=jj):
                        start_all(leave(jj))

                return carry

            lax.fori_loop(0, 8, one, 0)
            for j in range(4):
                outs += leave(j)
        wait_all(outs)

    full = lambda shape: pl.BlockSpec(shape, lambda i, s: (0,) * len(shape))
    out_shape, out_specs = [jax.ShapeDtypeStruct((length, cols), bf16)], [full((length, cols))]
    if blocks:
        out_shape += block_shapes(fw, cols, first_cols)
        out_specs += [ANY] * 5
    if whole:
        out_shape += [jax.ShapeDtypeStruct((length, D), bf16)] * 2
        out_specs += [ANY] * 2
    return pl.pallas_call(
        kernel,
        grid_spec=pltpu.PrefetchScalarGridSpec(
            num_scalar_prefetch=1,
            grid=(1,),
            in_specs=[ANY] * (len(a_src) + len(g_src) + 3 + len(arrays)),
            out_specs=out_specs,
            scratch_shapes=[
                pltpu.VMEM((length, D), bf16),
                pltpu.VMEM((length, D), bf16),
                pltpu.VMEM((D, n), bf16),
                pltpu.VMEM((D, n), bf16),
                pltpu.VMEM((n, dh), bf16),
                pltpu.VMEM((dh, n), bf16),
                pltpu.VMEM((length, n), f32),
                pltpu.VMEM((length, n), f32),
                pltpu.VMEM((4, 2 * fw, cols) if blocks else (1, 8, 128), bf16),
                pltpu.SemaphoreType.DMA((17,)),
            ],
        ),
        out_shape=out_shape,
        compiler_params=params(1),
        name="feed_first",
    )(scal, *a_src, *g_src, w_gate, w_up, w_down, *arrays)


def segments_length(sources):
    return sum(v.shape[0] for v in sources)


def feed_out(scal, kind, d, w_own, pieces, lo, hi, before, last):
    length = d.shape[0]
    n = hi - lo
    down = kind == "down"
    dh = w_own[0].shape[1] if down else w_own[0].shape[0]
    hidden = w_own[0].shape[0 if down else 1] // 2
    D = 2 * dh
    fw = dh // (lax.axis_size("dp") // 2)
    arrays = unique_arrays(pieces)
    ids = [2] if down else [0, 1]
    count = len(ids)
    split = [clip_pieces(pieces, i * n, (i + 1) * n) for i in ids]
    extra = [] if before is None else [before]

    def kernel(scal_ref, d_ref, *rest):
        own_refs, rest = rest[:count], rest[count:]
        piece_refs, rest = rest[: len(arrays)], rest[len(arrays) :]
        before_refs, rest = rest[: len(extra)], rest[len(extra) :]
        out_refs, rest = rest[: 2 if last else 1], rest[2 if last else 1 :]
        own_bufs, rest = rest[:count], rest[count:]
        oth_bufs, rest = rest[:count], rest[count:]
        d_buf, before_buf, sems = rest
        e, k = scal_ref[0], scal_ref[1]
        start = pl.multiple_of(k * hidden + lo, 128)
        own_copies, oth_copies = [], []
        for i in range(count):
            src = own_refs[i]
            src = src.at[pl.ds(start, n), :] if down else src.at[:, pl.ds(start, n)]
            own_copies.append(pltpu.make_async_copy(src, own_bufs[i], sems.at[2 * i]))
            oth_copies += piece_copies(
                split[i], arrays, piece_refs, oth_bufs[i], e, fw, sems.at[2 * i + 1]
            )
        d_copy = pltpu.make_async_copy(
            d_ref.at[:, pl.ds(ids[0] * n, count * n)], d_buf, sems.at[4]
        )
        d_copy.start()
        start_all(own_copies)
        before_copies = [pltpu.make_async_copy(ref, before_buf, sems.at[5]) for ref in before_refs]
        start_all(before_copies)
        start_all(oth_copies)
        d_copy.wait()

        def emit(value, cols):
            if extra:
                value = value + before_buf[:, cols]
            if last:
                split_store(value, out_refs[0], out_refs[1], cols)
            else:
                out_refs[0][:, cols] = value

        def own_cols(at, start):
            if down:
                value = mm(d_buf[...], own_bufs[0][:, at])
            else:
                value = mm_t(d_buf[:, :n], own_bufs[0][at, :])
                value = value + mm_t(d_buf[:, n:], own_bufs[1][at, :])
            emit(value, at)

        def oth_cols(at, start):
            value = mm_t(d_buf[:, :n], oth_bufs[0][at, :])
            if not down:
                value = value + mm_t(d_buf[:, n:], oth_bufs[1][at, :])
            emit(value, pl.ds(dh + start, WIDE))

        wait_all(own_copies)
        wait_all(before_copies)
        each_tile(dh, WIDE, own_cols)
        wait_all(oth_copies)
        each_tile(dh, WIDE, oth_cols)

    full = lambda shape: pl.BlockSpec(shape, lambda i, s: (0,) * len(shape))
    half = (length // 2, D)
    if last:
        out_shape = [jax.ShapeDtypeStruct(half, bf16), jax.ShapeDtypeStruct(half, f32)]
    else:
        out_shape = [jax.ShapeDtypeStruct((length, D), f32)]
    own_shape = (n, dh) if down else (dh, n)
    out = pl.pallas_call(
        kernel,
        grid_spec=pltpu.PrefetchScalarGridSpec(
            num_scalar_prefetch=1,
            grid=(1,),
            in_specs=[ANY] * (1 + count + len(arrays) + len(extra)),
            out_specs=[full(v.shape) for v in out_shape],
            scratch_shapes=[pltpu.VMEM(own_shape, bf16)] * count
            + [pltpu.VMEM((dh, n), bf16)] * count
            + [
                pltpu.VMEM((length, count * n), bf16),
                pltpu.VMEM((length, D) if extra else (8, 128), f32),
                pltpu.SemaphoreType.DMA((6,)),
            ],
        ),
        out_shape=out_shape,
        compiler_params=params(1),
    )(scal, d, *w_own, *arrays, *extra)
    return out if last else out[0]


def attend_grads(scal, groups, first_cols):
    _, D = groups[0][0].shape
    dh = D // 2
    fw = dh // 4
    lefts = []
    for left, _ in groups:
        if not any(left is v for v in lefts):
            lefts.append(left)
    picks = [[left is v for v in lefts].index(True) for left, _ in groups]
    rights = [right for _, right in groups]
    cols = sum(v.shape[1] for v in rights)

    def kernel(scal_ref, *rest):
        left_refs, rest = rest[: len(lefts)], rest[len(lefts) :]
        right_refs, rest = rest[: len(rights)], rest[len(rights) :]
        outs, (buf, sems) = rest[:5], rest[5:]
        e = scal_ref[0]

        def leave(j):
            return leave_block(buf, j, first_cols, outs, sems, 0)

        def one(i, carry):
            j, h = 3 - i // 2, i % 2
            at = pl.ds(pl.multiple_of(h * dh + (e ^ j) * fw, fw), fw)
            rows = pl.ds(pl.multiple_of(h * fw, fw), fw)
            col = 0
            for pick_at, right in zip(picks, right_refs):
                width = right.shape[1]
                value = t_mm(left_refs[pick_at][:, at], right[...]).astype(bf16)
                buf[j, rows, col : col + width] = value
                col += width
            for jj in range(4):

                @pl.when((j == jj) & (h == 1))
                def _(jj=jj):
                    start_all(leave(jj))

            return carry

        lax.fori_loop(0, 8, one, 0)
        for j in range(4):
            wait_all(leave(j))

    full = lambda shape: pl.BlockSpec(shape, lambda i, s: (0,) * len(shape))
    return pl.pallas_call(
        kernel,
        grid_spec=pltpu.PrefetchScalarGridSpec(
            num_scalar_prefetch=1,
            grid=(1,),
            in_specs=[full(v.shape) for v in lefts + rights],
            out_specs=[ANY] * 5,
            scratch_shapes=[
                pltpu.VMEM((4, 2 * fw, cols), bf16),
                pltpu.SemaphoreType.DMA((7,)),
            ],
        ),
        out_shape=block_shapes(fw, cols, first_cols),
        compiler_params=params(1),
        name="attend_grads",
    )(scal, *lefts, *rights)


def widen(v):
    return v.astype(f32)


def reduce_blocks(scal, blocks, first_cols, split=False):
    far_a, far_b, b1a, b2b, b0 = blocks
    rows = b0.shape[0]
    fw = rows // 2
    got_a = swap_chip(far_a, 1)
    got_b = swap_chip(far_b, 0)
    to_x = (widen(b1a) + widen(got_a[:rows])).astype(bf16)
    to_y = (widen(b2b) + widen(got_b[:rows])).astype(bf16)
    got_x = swap_chip(to_x, 0)
    got_y = swap_chip(to_y, 1)

    held = lax.optimization_barrier((b0, got_a, got_b, got_x, got_y))
    oth = sum_blocks(held, first_cols, slice(fw, rows), bf16)
    got_z = swap_row(oth)
    if split:
        return finish_span(scal, (b0, got_a, got_b, got_x, got_y, got_z), first_cols)
    parts = lax.optimization_barrier((b0, got_a, got_b, got_x, got_y, got_z))
    return sum_blocks(parts, first_cols, slice(0, fw), f32) + widen(parts[5])


def finish_span(scal, parts, first_cols):
    b0 = parts[0]
    cols = b0.shape[1]
    fw, n = b0.shape[0] // 2, cols // 3
    half = fw // 2

    def kernel(scal_ref, b0_ref, a_ref, b_ref, x_ref, y_ref, z_ref, mine_ref, theirs_ref, down_ref, total):
        k = scal_ref[1]
        total[:, :first_cols] = widen(b0_ref[:, :first_cols]) + widen(a_ref[...]) + widen(x_ref[...])
        total[:, first_cols:] = widen(b0_ref[:, first_cols:]) + widen(b_ref[...]) + widen(y_ref[...])
        total[...] += widen(z_ref[...])
        here = pl.ds(pl.multiple_of(k * half, half), half)
        away = pl.ds(pl.multiple_of((1 - k) * half, half), half)
        mine_ref[...] = total[here, : 2 * n]
        theirs_ref[...] = total[away, : 2 * n]
        down_ref[...] = total[:, 2 * n :].astype(bf16)

    def rows(v, at):
        return pl.BlockSpec((fw, v.shape[1]), lambda i, s: (at, 0))

    full = lambda shape: pl.BlockSpec(shape, lambda i, s: (0,) * len(shape))
    out_shape = [
        jax.ShapeDtypeStruct((half, 2 * n), f32),
        jax.ShapeDtypeStruct((half, 2 * n), f32),
        jax.ShapeDtypeStruct((fw, n), bf16),
    ]
    return pl.pallas_call(
        kernel,
        grid_spec=pltpu.PrefetchScalarGridSpec(
            num_scalar_prefetch=1,
            grid=(1,),
            in_specs=[rows(v, at) for v, at in zip(parts, (0, 2, 2, 0, 0, 0))],
            out_specs=[full(v.shape) for v in out_shape],
            scratch_shapes=[pltpu.VMEM((fw, cols), f32)],
        ),
        out_shape=out_shape,
        compiler_params=params(1),
        name="finish_span",
    )(scal, *parts)


def join_spans(scal, spans, mine, theirs):
    hidden = sum(v.shape[1] for v in mine) // 2
    count = len(spans)

    def kernel(scal_ref, *rest):
        outs, sems = rest[2 * count : 2 * count + 2], rest[-1]
        k = scal_ref[1]
        copies = []
        for side in range(2):
            core = k if side == 0 else 1 - k
            for i, (lo, hi) in enumerate(spans):
                ref, n = rest[side * count + i], hi - lo
                at = pl.ds(pl.multiple_of(core * hidden + lo, 128), n)
                for which in range(2):
                    copies.append(
                        pltpu.make_async_copy(
                            ref.at[:, pl.ds(which * n, n)],
                            outs[which].at[:, at],
                            sems.at[len(copies)],
                        )
                    )
        start_all(copies)
        wait_all(copies)

    full = lambda shape: pl.BlockSpec(shape, lambda i, s: (0,) * len(shape))
    shape = jax.ShapeDtypeStruct((mine[0].shape[0], 2 * hidden), f32)
    return pl.pallas_call(
        kernel,
        grid_spec=pltpu.PrefetchScalarGridSpec(
            num_scalar_prefetch=1,
            grid=(1,),
            in_specs=[full(v.shape) for v in mine + theirs],
            out_specs=[ANY] * 2,
            scratch_shapes=[pltpu.SemaphoreType.DMA((4 * count,))],
        ),
        out_shape=[shape] * 2,
        compiler_params=params(1),
        name="join_spans",
    )(scal, *mine, *theirs)


def sum_blocks(parts, first_cols, part, kind):
    b0, got_a, got_b, got_x, got_y = parts[:5]
    rows = b0.shape[0]
    left = widen(b0[part, :first_cols]) + widen(got_a[rows:][part]) + widen(got_x[part])
    right = widen(b0[part, first_cols:]) + widen(got_b[rows:][part]) + widen(got_y[part])
    return jnp.concatenate([left.astype(kind), right.astype(kind)], 1)


def reduce_groups(e, groups):
    chips = lax.axis_size("dp") // 2
    nbits = chips.bit_length() - 1
    dh = groups[0][0].shape[1] // 2

    def make(keys):
        outs = []
        for left, right in groups:
            left = jnp.concatenate(
                [xor_axis(left[:, :dh], e, 1, chips), xor_axis(left[:, dh:], e, 1, chips)], 1
            )
            left = take_keys(left, list(range(chips)), keys, 1)
            outs.append(t_mm(left, right))
        return jnp.concatenate(outs, 1)

    return reduce_features(make, list(range(nbits)), 0)


def tp_finish(send, keep):
    got = swap_core(send)
    half = keep.shape[0] // 2
    away = (keep[half:] + widen(got[half:])).astype(bf16)
    mate = swap_col(away)
    return keep[:half] + widen(got[:half]) + widen(mate)


def on_device(
    tokens,
    segments,
    positions,
    attn_gain,
    w_query,
    w_key,
    w_value,
    w_out,
    mlp_gain,
    w_gate,
    w_up,
    w_down,
    cotangent,
):
    dp = lax.axis_index("dp")
    e, k = dp >> 1, dp & 1
    r, c = lax.axis_index("row"), lax.axis_index("col")
    chips = lax.axis_size("dp") // 2
    nbits = chips.bit_length() - 1
    scal = jnp.stack([e, k, c]).astype(jnp.int32)
    diag = k == r
    length = segments.shape[1]
    blk = length // 4
    dh = tokens.shape[2]
    D = 2 * dh
    fw = dh // chips
    nq = w_query.shape[1] // 2
    hidden = w_gate.shape[1] // 2
    first, second = side_perms()

    def spread_in(v):
        parts = v[0].reshape(2, blk, dh)
        here = jnp.where(r == 0, parts[0], parts[1])
        away = jnp.where(r == 0, parts[1], parts[0])
        here, away = lax.optimization_barrier((here, away))
        got_a = lax.ppermute(away, ("dp", "row"), first)
        got_b = lax.ppermute(here, ("dp", "row"), second)
        own = jnp.where(diag, here, got_a)
        oth = jnp.where(diag, got_a, got_b)
        return jnp.concatenate([own, oth], 1)

    def spread_out(v):
        own, oth = v[:, :dh], v[:, dh:]
        mixed = jnp.where(diag, oth, own)
        own, oth, mixed = lax.optimization_barrier((own, oth, mixed))
        got_a = lax.ppermute(mixed, ("dp", "row"), flip(first))
        got_b = lax.ppermute(oth, ("dp", "row"), flip(second))

        here = jnp.where(diag, own, got_b)
        return order_pair(here, got_a, r, 0)[None]

    gains = jnp.stack([attn_gain, mlp_gain])
    got_gains = swap_row(gains)
    meta = jnp.concatenate([segments, positions], 0)
    meta = jnp.where(diag, meta, swap_core(meta))
    marks_t = meta[:1]
    marks = marks_t.T
    quarter = jnp.split(meta[1:], 4, 1)
    order = xor_blocks([quarter[0], quarter[2], quarter[1], quarter[3]], 2 * k + c)
    place = jnp.concatenate(order, 1)[0]
    half = HD // 2
    frequency = 10000.0 ** (-jnp.arange(half, dtype=f32) * 2.0 / HD)
    angles = place.astype(f32)[:, None] * frequency[None, :]
    cosine, sine = jnp.cos(angles), jnp.sin(angles)
    cosine = jnp.concatenate([cosine] * 4, 1)
    sine = jnp.concatenate([-sine, sine] * 2, 1)

    x = spread_in(tokens)
    wkv = jnp.concatenate([pick(w_key, k, 1), pick(w_value, k, 1)], 1)

    def rows_shard(w, start, size):
        return lax.dynamic_slice(w, (e * fw, start), (fw, size))

    def cols_shard(w, start, size):
        return lax.dynamic_slice(w, (start, e * fw), (size, fw)).T

    parts = [rows_shard(w_query, k * nq, nq), rows_shard(wkv, 0, 128), cols_shard(w_out, k * nq, nq)]
    shard = jnp.concatenate(parts, 1)
    attn_pieces = gather_unit(swap_row(shard), 640)
    g = spread_in(cotangent)
    spans = [(0, 512), (512, 1024), (1024, hidden)]
    feed_pieces = []
    for lo, hi in spans:
        n = hi - lo
        at = k * hidden + lo
        parts = [rows_shard(w_gate, at, n), rows_shard(w_up, at, n), cols_shard(w_down, at, n)]
        groups = [(parts, 0)]
        pieces = []
        for group, col in groups:
            group = lax.optimization_barrier(group)
            shard = jnp.concatenate(group, 1)
            cut_at = shard.shape[1] // 256 * 128
            pieces += gather_unit(swap_row(shard), cut_at, col)
        feed_pieces.append(pieces)

    x, got_gains, gains = lax.optimization_barrier((x, got_gains, gains))
    gains = jnp.concatenate([gains, got_gains], 1)
    xf = x.astype(f32)
    r1 = lax.rsqrt(jnp.sum(xf * xf, axis=1, keepdims=True) / D + epsilon)
    a1 = (xf * r1 * gains[0]).astype(bf16)
    a1 = tp_gather(a1)
    q, kdup, vdup, o, send, keep, a1 = attend_forward(
        scal, a1, w_query, wkv, w_out, attn_pieces, cosine, sine, marks, marks_t
    )
    hres = xf + tp_finish(send, keep)
    r2 = lax.rsqrt(jnp.sum(hres * hres, axis=1, keepdims=True) / D + epsilon)
    a2 = (hres * r2 * gains[1]).astype(bf16)
    a2 = tp_gather(a2)
    g_all = tp_gather(g)

    out_part, da2_part = None, None
    feed_sums = []
    for i, ((lo, hi), pieces) in enumerate(zip(spans, feed_pieces)):
        last = i == len(spans) - 1
        n = hi - lo
        cut_at = 3 * n // 256 * 128
        outs = feed_first(scal, a2, g_all, w_gate, w_up, w_down, pieces, lo, hi, cut_at)
        d, outs = outs[0], outs[1:]
        if i == 0:
            a2, g_all = [outs[-2]], [outs[-1]]
        da2_part = feed_out(scal, "in", d, [w_gate, w_up], pieces, lo, hi, da2_part, last)
        if chips == 4:
            feed_sums.append(reduce_blocks(scal, outs[:5], cut_at, True))
        else:
            groups = [(a2[0], d[:, : 2 * n]), (g_all[0], d[:, 2 * n :])]
            feed_sums.append(reduce_groups(e, groups))
        out_part = feed_out(scal, "down", d, [w_down], pieces, lo, hi, out_part, last)
    kept, sent, keep = lax.optimization_barrier((hres, *out_part))
    result = tp_finish(sent, keep)
    result = (kept + result).astype(bf16)
    result = spread_out(result)

    def norm_back(inputs, factor, gain, upstream):
        weighted = upstream * gain
        dotted = jnp.sum(weighted * inputs, axis=1, keepdims=True)
        grad = factor * weighted - inputs * factor**3 * dotted / D
        return grad, jnp.sum(upstream * inputs * factor, axis=0)

    da2 = tp_finish(*da2_part)
    dh_grad, gain_two = norm_back(hres, r2, gains[1], da2)
    dh_grad = dh_grad + widen(g)
    dz = dh_grad.astype(bf16)
    dz = tp_gather(dz)
    dq, dkv, send, keep, dz = attend_backward(
        scal, dz, q, kdup, vdup, w_query, wkv, w_out, attn_pieces, cosine, sine, marks, marks_t
    )
    if chips == 4:
        o_blocks = attend_grads(scal, [(dz, o)], 256)
        q_blocks = attend_grads(scal, [(a1, dq), (a1, dkv)], 256)
        out_sum = reduce_blocks(scal, o_blocks, 256)
        qkv_sum = reduce_blocks(scal, q_blocks, 256)
    else:
        attn_sum = reduce_groups(e, [(a1, jnp.concatenate([dq, dkv], 1)), (dz, o)])
        qkv_sum, out_sum = attn_sum[:, : nq + 128], attn_sum[:, nq + 128 :]
    da1 = tp_finish(send, keep)
    grad_x, gain_one = norm_back(xf, r1, gains[0], da1)
    grad_x = (grad_x + dh_grad).astype(bf16)
    grad_x = spread_out(grad_x)

    both = jnp.stack([gain_one, gain_two])
    both = both + swap_core(both)
    for bit in range(nbits):
        both = both + swap_chip(both, bit)
    both = both + swap_col(both)
    own = both[:, :dh] + swap_row(both[:, dh:])

    def rows_home(v):
        return pick(v, k, 0), swap_core(pick(v, 1 - k, 0))

    if chips == 4:
        mines = [v[0] for v in feed_sums]
        others = [swap_core(v[1]) for v in feed_sums]
        grad_gate, grad_up = join_spans(scal, spans, mines, others)
        downs = [v[2] for v in feed_sums]
    else:
        homes = []
        for (lo, hi), v in zip(spans, feed_sums):
            homes.append(rows_home(v[:, : 2 * (hi - lo)]))
        grads = []
        for which in range(2):
            sides = []
            for side in range(2):
                for (lo, hi), home in zip(spans, homes):
                    n = hi - lo
                    sides.append(home[side][:, which * n : (which + 1) * n])
            mine = jnp.concatenate(sides[: len(spans)], 1)
            theirs = jnp.concatenate(sides[len(spans) :], 1)
            grads.append(order_pair(mine, theirs, k, 1))
        grad_gate, grad_up = grads
        downs = [v[:, 2 * (hi - lo) :] for (lo, hi), v in zip(spans, feed_sums)]
    mine, theirs = rows_home(qkv_sum)
    grad_query = order_pair(mine[:, :nq], theirs[:, :nq], k, 1)
    grad_key = order_pair(mine[:, nq : nq + HD], theirs[:, nq : nq + HD], k, 1)
    grad_value = order_pair(mine[:, nq + HD :], theirs[:, nq + HD :], k, 1)

    def exchange(sums):
        views = []
        for v in sums:
            v = v.astype(bf16).T
            views.append(v.reshape(chips // 2, 2, v.shape[0] // chips, v.shape[1]))
        view = jnp.concatenate(views, 2)
        mine = jnp.where(k == 0, view[:, 0], view[:, 1])
        got = swap_core(jnp.where(k == 0, view[:, 1], view[:, 0]))
        full = order_pair(mine, got, k, 0)
        rel = xor_blocks([full[i] for i in range(chips)], e)
        n = lax.axis_size("dp")
        out = [rel[0]]
        for j in range(1, chips):
            out.append(lax.ppermute(rel[j], "dp", [(i, i ^ (2 * j)) for i in range(n)]))
        cut_at = views[0].shape[2]
        whole = xor_blocks(out, e)
        return [
            jnp.concatenate([v[part] for v in whole], 1).astype(f32)
            for part in (slice(0, cut_at), slice(cut_at, None))
        ]

    grad_down, grad_out = exchange([jnp.concatenate(downs, 1), out_sum])
    return (
        result,
        grad_x,
        own[0],
        grad_query[None],
        grad_key[None],
        grad_value[None],
        grad_out[None],
        own[1],
        grad_gate[None],
        grad_up[None],
        grad_down[None],
    )


def solution(mesh):
    placed = (
        P("dp", "col", "row"),
        P("dp", None),
        P("dp", None),
        P("row"),
        P("row", "col"),
        P("row", "col"),
        P("row", "col"),
        P("col", "row"),
        P("row"),
        P("row", "col"),
        P("row", "col"),
        P("col", "row"),
        P("dp", "col", "row"),
    )
    return jax.shard_map(
        on_device,
        mesh=mesh,
        in_specs=placed,
        out_specs=(
            P("dp", "col", "row"),
            P("dp", "col", "row"),
            P("row"),
            P("row", "dp", "col"),
            P("row", "dp", "col"),
            P("row", "dp", "col"),
            P("col", "dp", "row"),
            P("row"),
            P("row", "dp", "col"),
            P("row", "dp", "col"),
            P("col", "dp", "row"),
        ),
        check_vma=False,
    )
```

```python
import jax
import jax.numpy as jnp
from jax import lax
from jax.experimental import pallas as pl
from jax.experimental.pallas import tpu as pltpu
from jax.sharding import PartitionSpec as P


HD = 64
epsilon = 1e-05
masked_score = -1e30
f32 = jnp.float32
bf16 = jnp.bfloat16


def swap_core(v):
    n = lax.axis_size("dp")
    return lax.ppermute(v, "dp", [(i, i ^ 1) for i in range(n)])


def swap_chip(v, bit):
    n = lax.axis_size("dp")
    return lax.ppermute(v, "dp", [(i, i ^ (2 << bit)) for i in range(n)])


def swap_row(v):
    return lax.ppermute(v, "row", [(0, 1), (1, 0)])


def swap_col(v):
    return lax.ppermute(v, "col", [(0, 1), (1, 0)])


def side_perms():
    chips = lax.axis_size("dp") // 2
    first, second = [], []
    for e in range(chips):
        for a in range(2):
            same = (2 * e + a) * 2 + a
            other = (2 * e + a) * 2 + 1 - a
            mate = (2 * e + 1 - a) * 2 + a
            first += [(same, mate), (other, same)]
            second += [(other, mate)]
    return first, second


def flip(perm):
    return [(b, a) for a, b in perm]


def xor_blocks(blocks, index):
    bit = 0
    while (1 << bit) < len(blocks):
        on = ((index >> bit) & 1) == 1
        blocks = [jnp.where(on, blocks[i ^ (1 << bit)], blocks[i]) for i in range(len(blocks))]
        bit += 1
    return blocks


def xor_axis(v, index, axis, count):
    return jnp.concatenate(xor_blocks(jnp.split(v, count, axis), index), axis)


def pick(v, index, axis):
    lo, hi = jnp.split(v, 2, axis)
    return jnp.where(index == 0, lo, hi)


def order_pair(mine, theirs, index, axis):
    return jnp.where(
        index == 0,
        jnp.concatenate([mine, theirs], axis),
        jnp.concatenate([theirs, mine], axis),
    )


def mm(a, b):
    return jnp.dot(a, b, preferred_element_type=f32)


def mm_t(a, b):
    return lax.dot_general(a, b, (((1,), (1,)), ((), ())), preferred_element_type=f32)


def t_mm(a, b):
    return lax.dot_general(a, b, (((0,), (0,)), ((), ())), preferred_element_type=f32)


def tp_gather(v):
    mate = swap_col(v)
    return [v, mate, swap_core(v), swap_core(mate)]


def gather_chips(shard, bits, axis):
    held = {0: shard}
    for bit in bits:
        keys = list(held)
        got = swap_chip(jnp.concatenate([held[j] for j in keys], axis), bit)
        for j, piece in zip(keys, jnp.split(got, len(keys), axis)):
            held[j ^ (1 << bit)] = piece
    return jnp.concatenate([held[j] for j in range(len(held))], axis)


def cut(v, start, size, axis):
    return lax.slice_in_dim(v, start, start + size, axis=axis)


def take_keys(v, have, want, axis):
    width = v.shape[axis] // (2 * len(have))
    out = []
    for h in range(2):
        for j in want:
            out.append(cut(v, (h * len(have) + have.index(j)) * width, width, axis))
    return out[0] if len(out) == 1 else jnp.concatenate(out, axis)


def reduce_features(make, bits, axis):
    count = 1 << len(bits)
    keys = list(range(count))
    got = []

    def total(want):
        value = make(want)
        for have, arr in got:
            value = value + take_keys(arr, have, want, axis).astype(f32)
        return value

    for bit in bits:
        send = [j for j in keys if (j >> bit) & 1]
        keys = [j for j in keys if not (j >> bit) & 1]
        arr = swap_chip(total(send).astype(bf16), bit)
        got.append(([j ^ (1 << bit) for j in send], arr))
    own, other = jnp.split(total(keys), 2, axis)
    return own + swap_row(other.astype(bf16)).astype(f32)


ANY = pl.BlockSpec(memory_space=pl.ANY)
LIMIT = 60 << 20


def params(dims):
    return pltpu.CompilerParams(
        dimension_semantics=("arbitrary",) * dims, vmem_limit_bytes=LIMIT
    )


def gather_unit(shard, first_cols, at=0):
    chips = lax.axis_size("dp") // 2
    rows, cols = shard.shape
    if chips == 4:
        got_x, got_y = swap_chip(shard, 0), swap_chip(shard, 1)
        far_a = swap_chip(got_x[:, :first_cols], 1)
        far_b = swap_chip(got_y[:, first_cols:], 0)
        return [
            (shard, 0, 0, 0, cols, at),
            (got_x, 0, 1, 0, cols, at),
            (got_y, 0, 2, 0, cols, at),
            (far_a, 0, 3, 0, first_cols, at),
            (far_b, 0, 3, 0, cols - first_cols, at + first_cols),
        ]
    nbits = chips.bit_length() - 1
    whole = gather_chips(shard, list(range(nbits)), 0)
    return [(whole, j * rows, j, 0, cols, at) for j in range(chips)]


def clip_pieces(pieces, lo, hi):
    out = []
    for array, row, j, col, count, at in pieces:
        a, b = max(lo, at), min(hi, at + count)
        if a < b:
            out.append((array, row, j, col + a - at, b - a, a - lo))
    return out


def unique_arrays(pieces):
    arrays = []
    for piece in pieces:
        if not any(piece[0] is a for a in arrays):
            arrays.append(piece[0])
    return arrays


def piece_copies(pieces, arrays, refs, target, e, fw, sem):
    copies = []
    for array, row, j, col, count, at in pieces:
        ref = refs[[a is array for a in arrays].index(True)]
        copies.append(
            pltpu.make_async_copy(
                ref.at[pl.ds(row, fw), pl.ds(col, count)],
                target.at[pl.ds(pl.multiple_of((e ^ j) * fw, fw), fw), pl.ds(at, count)],
                sem,
            )
        )
    return copies


def start_all(copies):
    for copy in copies:
        copy.start()


def wait_all(copies):
    for copy in copies:
        copy.wait()


def lanes_low(shape):
    return lax.broadcasted_iota(jnp.int32, shape, 1) % 128 < HD


def turn(x, cosine, sine):
    lane = lax.broadcasted_iota(jnp.int32, x.shape, 1) % HD
    mate = jnp.where(lane < HD // 2, pltpu.roll(x, 128 - HD // 2, 1), pltpu.roll(x, HD // 2, 1))
    return x * cosine + mate * sine


def place_of(scal_ref, i, blk):
    k, c = scal_ref[1], scal_ref[2]
    local = ((i & 1) ^ k) * 2 + ((i >> 1) ^ c)
    return pl.ds(pl.multiple_of(local * blk, blk), blk)


def fill_bias(bias, mk_ref, mt_ref):
    shape = bias.shape
    before = lax.broadcasted_iota(jnp.int32, shape, 0) >= lax.broadcasted_iota(jnp.int32, shape, 1)
    bias[...] = jnp.where((mk_ref[...] == mt_ref[...]) & before, 0.0, masked_score)


def two_heads(x):
    low = lanes_low(x.shape)
    zero = jnp.zeros(x.shape, x.dtype)
    return jnp.concatenate([jnp.where(low, x, zero), jnp.where(low, zero, x)], 0)


def one_row(x):
    rows = x.shape[0] // 2
    return jnp.where(lanes_low((rows, x.shape[1])), x[:rows], x[rows:])


def softmax_rows(qm, kdup, bias, scale):
    scores = mm_t(qm, kdup) * scale + jnp.concatenate([bias, bias], 0)
    top = jnp.max(scores, axis=1, keepdims=True)
    weights = jnp.exp(scores - top)
    return weights * (1.0 / jnp.sum(weights, axis=1, keepdims=True))


def split_store(value, send_ref, keep_ref, cols):
    half = value.shape[0] // 2
    keep_ref[:, cols] = value[:half]
    send_ref[:, cols] = value[half:].astype(bf16)


def attend_forward(scal, a_src, w_query, wkv, w_out, pieces, cosine, sine, marks, marks_t):
    length, D = segments_length(a_src), a_src[0].shape[1]
    dh = w_query.shape[0]
    nq = w_query.shape[1] // 2
    pairs = nq // 128
    fw = dh // (lax.axis_size("dp") // 2)
    qkv_pieces = clip_pieces(pieces, 0, nq + 128)
    out_pieces = clip_pieces(pieces, nq + 128, 2 * nq + 128)
    arrays = unique_arrays(pieces)
    scale = HD ** (-0.5)
    blk = length // 4

    def kernel(scal_ref, *rest):
        a_refs, rest = rest[: len(a_src)], rest[len(a_src) :]
        (wq_ref, wkv_ref, wo_ref, cos_ref, sin_ref, mk_ref, mt_ref), rest = rest[:7], rest[7:]
        piece_refs = rest[: len(arrays)]
        q_ref, kdup_ref, vdup_ref, o_ref, send_ref, keep_ref, a_out = rest[len(arrays) : len(arrays) + 7]
        a_ref, wq, woth, wo, wot, qkv, kloc, vloc, bias, attended, sems = rest[len(arrays) + 7 :]
        e, k = scal_ref[0], scal_ref[1]
        step = pl.program_id(0)

        def first_copies():
            own = pltpu.make_async_copy(
                wq_ref.at[:, pl.ds(pl.multiple_of(k * nq, nq), nq)], wq, sems.at[0]
            )
            return [own] + piece_copies(qkv_pieces, arrays, piece_refs, woth, e, fw, sems.at[1])

        def later_copies():
            own = pltpu.make_async_copy(
                wo_ref.at[pl.ds(pl.multiple_of(k * nq, nq), nq), :], wo, sems.at[2]
            )
            return [own] + piece_copies(out_pieces, arrays, piece_refs, wot, e, fw, sems.at[3])

        @pl.when(step == 0)
        def _():
            copies = gather_tokens(a_refs, a_ref, sems.at[4]) + first_copies()
            start_all(copies)
            start_all(later_copies())
            fill_bias(bias, mk_ref, mt_ref)
            wait_all(copies)
            pltpu.make_async_copy(a_ref, a_out, sems.at[5]).start()
            a_own, a_oth = a_ref[:, :dh], a_ref[:, dh:]
            qkv[:, :nq] = mm(a_own, wq[...]) + mm(a_oth, woth[:, :nq])
            kv = mm(a_own, wkv_ref[...]) + mm(a_oth, woth[:, nq:])
            low = lanes_low(kv.shape)
            kv = jnp.where(low, turn(kv, cos_ref[...], sin_ref[...]), kv)
            swapped = pltpu.roll(kv, HD, 1)
            kloc[...] = jnp.where(low, kv, swapped)
            vloc[...] = jnp.where(low, swapped, kv)
            for i in range(4):
                rows = place_of(scal_ref, i, blk)
                kdup_ref[i * blk : (i + 1) * blk, :] = kloc[rows, :].astype(bf16)
                vdup_ref[i * blk : (i + 1) * blk, :] = vloc[rows, :].astype(bf16)

        at = pl.ds(pl.multiple_of(step * 128, 128), 128)
        q = turn(qkv[:, at], cos_ref[...], sin_ref[...]).astype(bf16)
        q_ref[...] = q
        for i in range(4):
            rows = place_of(scal_ref, i, blk)
            keys = (i + 1) * blk
            mask = bias[i * blk : keys, :keys]
            probs = softmax_rows(two_heads(q_ref[rows, :]), kdup_ref[:keys, :], mask, scale)
            value = one_row(mm(probs.astype(bf16), vdup_ref[:keys, :])).astype(bf16)
            o_ref[rows, :] = value
            attended[rows, at] = value

        @pl.when(step == pairs - 1)
        def _():
            wait_all(later_copies() + [pltpu.make_async_copy(a_ref, a_out, sems.at[5])])
            o = attended[...]
            split_store(mm(o, wo[...]), send_ref, keep_ref, slice(0, dh))
            split_store(mm_t(o, wot[...]), send_ref, keep_ref, slice(dh, D))

    full = lambda shape: pl.BlockSpec(shape, lambda i, s: (0,) * len(shape))
    return pl.pallas_call(
        kernel,
        grid_spec=pltpu.PrefetchScalarGridSpec(
            num_scalar_prefetch=1,
            grid=(pairs,),
            in_specs=[ANY] * len(a_src)
            + [ANY, full(wkv.shape), ANY]
            + [full(v.shape) for v in (cosine, sine, marks, marks_t)]
            + [ANY] * len(arrays),
            out_specs=[
                pl.BlockSpec((length, 128), lambda i, s: (0, i)),
                full((length, 128)),
                full((length, 128)),
                pl.BlockSpec((length, 128), lambda i, s: (0, i)),
                full((length // 2, D)),
                full((length // 2, D)),
                ANY,
            ],
            scratch_shapes=[
                pltpu.VMEM((length, D), bf16),
                pltpu.VMEM((dh, nq), bf16),
                pltpu.VMEM((dh, nq + 128), bf16),
                pltpu.VMEM((nq, dh), bf16),
                pltpu.VMEM((dh, nq), bf16),
                pltpu.VMEM((length, nq), f32),
                pltpu.VMEM((length, 128), f32),
                pltpu.VMEM((length, 128), f32),
                pltpu.VMEM((length, length), f32),
                pltpu.VMEM((length, nq), bf16),
                pltpu.SemaphoreType.DMA((6,)),
            ],
        ),
        out_shape=[
            jax.ShapeDtypeStruct((length, nq), bf16),
            jax.ShapeDtypeStruct((length, 128), bf16),
            jax.ShapeDtypeStruct((length, 128), bf16),
            jax.ShapeDtypeStruct((length, nq), bf16),
            jax.ShapeDtypeStruct((length // 2, D), bf16),
            jax.ShapeDtypeStruct((length // 2, D), f32),
            jax.ShapeDtypeStruct((length, D), bf16),
        ],
        compiler_params=params(1),
        name="attend_forward",
    )(scal, *a_src, w_query, wkv, w_out, cosine, sine, marks, marks_t, *arrays)


def attend_backward(scal, z_src, q, kdup, vdup, w_query, wkv, w_out, pieces, cosine, sine, marks, marks_t):
    length, D = segments_length(z_src), z_src[0].shape[1]
    dh = w_query.shape[0]
    nq = w_query.shape[1] // 2
    pairs = nq // 128
    fw = dh // (lax.axis_size("dp") // 2)
    qkv_pieces = clip_pieces(pieces, 0, nq + 128)
    out_pieces = clip_pieces(pieces, nq + 128, 2 * nq + 128)
    arrays = unique_arrays(pieces)
    scale = HD ** (-0.5)
    blk = length // 4

    def kernel(scal_ref, *rest):
        z_refs, rest = rest[: len(z_src)], rest[len(z_src) :]
        q_ref, kdup_ref, vdup_ref, wq_ref, wkv_ref, wo_ref = rest[:6]
        (cos_ref, sin_ref, mk_ref, mt_ref), rest = rest[6:10], rest[10:]
        piece_refs = rest[: len(arrays)]
        dq_ref, dkv_ref, send_ref, keep_ref, z_out = rest[len(arrays) : len(arrays) + 5]
        dz_ref, wq, woth, wo, wot, do, bias, dqs, dk, dv, sems = rest[len(arrays) + 5 :]
        e, k = scal_ref[0], scal_ref[1]
        step = pl.program_id(0)

        def first_copies():
            own = pltpu.make_async_copy(
                wo_ref.at[pl.ds(pl.multiple_of(k * nq, nq), nq), :], wo, sems.at[2]
            )
            return [own] + piece_copies(out_pieces, arrays, piece_refs, wot, e, fw, sems.at[3])

        def later_copies():
            own = pltpu.make_async_copy(
                wq_ref.at[:, pl.ds(pl.multiple_of(k * nq, nq), nq)], wq, sems.at[0]
            )
            return [own] + piece_copies(qkv_pieces, arrays, piece_refs, woth, e, fw, sems.at[1])

        @pl.when(step == 0)
        def _():
            copies = gather_tokens(z_refs, dz_ref, sems.at[4]) + first_copies()
            start_all(copies)
            start_all(later_copies())
            fill_bias(bias, mk_ref, mt_ref)
            dk[...] = jnp.zeros_like(dk)
            dv[...] = jnp.zeros_like(dv)
            wait_all(copies)
            pltpu.make_async_copy(dz_ref, z_out, sems.at[5]).start()
            do[...] = (mm_t(dz_ref[:, :dh], wo[...]) + mm(dz_ref[:, dh:], wot[...])).astype(bf16)

        at = pl.ds(pl.multiple_of(step * 128, 128), 128)
        for i in range(4):
            rows = place_of(scal_ref, i, blk)
            keys = (i + 1) * blk
            mask = bias[i * blk : keys, :keys]
            kd, vd = kdup_ref[:keys, :], vdup_ref[:keys, :]
            qm, dom = two_heads(q_ref[rows, :]), two_heads(do[rows, at])
            probs = softmax_rows(qm, kd, mask, scale)
            dprob = mm_t(dom, vd)
            centre = jnp.sum(probs * dprob, axis=1, keepdims=True)
            ds = (probs * (dprob - centre) * scale).astype(bf16)
            dv[:keys, :] += t_mm(probs.astype(bf16), dom)
            dk[:keys, :] += t_mm(ds, qm)
            value = turn(one_row(mm(ds, kd)), cos_ref[rows, :], -sin_ref[rows, :]).astype(bf16)
            dq_ref[rows, :] = value
            dqs[rows, at] = value

        @pl.when(step == pairs - 1)
        def _():
            for i in range(4):
                rows = place_of(scal_ref, i, blk)
                part = slice(i * blk, (i + 1) * blk)
                dks = dk[part, :] + pltpu.roll(dk[part, :], HD, 1)
                dvs = dv[part, :] + pltpu.roll(dv[part, :], HD, 1)
                dks = turn(dks, cos_ref[rows, :], -sin_ref[rows, :])
                dkv_ref[rows, :] = jnp.where(lanes_low(dks.shape), dks, dvs).astype(bf16)
            dkv = dkv_ref[...]
            wait_all(later_copies() + [pltpu.make_async_copy(dz_ref, z_out, sems.at[5])])
            dq_all = dqs[...]
            own = mm_t(dq_all, wq[...]) + mm_t(dkv, wkv_ref[...])
            split_store(own, send_ref, keep_ref, slice(0, dh))
            oth = mm_t(dq_all, woth[:, :nq]) + mm_t(dkv, woth[:, nq:])
            split_store(oth, send_ref, keep_ref, slice(dh, D))

    full = lambda shape: pl.BlockSpec(shape, lambda i, s: (0,) * len(shape))
    return pl.pallas_call(
        kernel,
        grid_spec=pltpu.PrefetchScalarGridSpec(
            num_scalar_prefetch=1,
            grid=(pairs,),
            in_specs=[ANY] * len(z_src)
            + [
                pl.BlockSpec((length, 128), lambda i, s: (0, i)),
                full(kdup.shape),
                full(vdup.shape),
                ANY,
                full(wkv.shape),
                ANY,
            ]
            + [full(v.shape) for v in (cosine, sine, marks, marks_t)]
            + [ANY] * len(arrays),
            out_specs=[
                pl.BlockSpec((length, 128), lambda i, s: (0, i)),
                full((length, 128)),
                full((length // 2, D)),
                full((length // 2, D)),
                ANY,
            ],
            scratch_shapes=[
                pltpu.VMEM((length, D), bf16),
                pltpu.VMEM((dh, nq), bf16),
                pltpu.VMEM((dh, nq + 128), bf16),
                pltpu.VMEM((nq, dh), bf16),
                pltpu.VMEM((dh, nq), bf16),
                pltpu.VMEM((length, nq), bf16),
                pltpu.VMEM((length, length), f32),
                pltpu.VMEM((length, nq), bf16),
                pltpu.VMEM((length, 128), f32),
                pltpu.VMEM((length, 128), f32),
                pltpu.SemaphoreType.DMA((6,)),
            ],
        ),
        out_shape=[
            jax.ShapeDtypeStruct((length, nq), bf16),
            jax.ShapeDtypeStruct((length, 128), bf16),
            jax.ShapeDtypeStruct((length // 2, D), bf16),
            jax.ShapeDtypeStruct((length // 2, D), f32),
            jax.ShapeDtypeStruct((length, D), bf16),
        ],
        compiler_params=params(1),
        name="attend_backward",
    )(scal, *z_src, q, kdup, vdup, w_query, wkv, w_out, cosine, sine, marks, marks_t, *arrays)


def tiles_of(n, width):
    return [(lo, min(n, lo + width)) for lo in range(0, n, width)]


def gather_tokens(sources, target, sem):
    if len(sources) == 1:
        return [pltpu.make_async_copy(sources[0], target, sem)]
    blk = target.shape[0] // len(sources)
    return [
        pltpu.make_async_copy(source, target.at[pl.ds(i * blk, blk), :], sem)
        for i, source in enumerate(sources)
    ]


def leave_block(buf, j, first_cols, outs, sems, base):
    far_a, far_b, b1a, b2b, b0 = outs
    rows, cols = buf.shape[1], buf.shape[2]
    left = buf.at[j, :, pl.ds(0, first_cols)]
    right = buf.at[j, :, pl.ds(first_cols, cols - first_cols)]
    copy = pltpu.make_async_copy
    if j == 3:
        return [
            copy(left, far_a.at[pl.ds(0, rows), :], sems.at[base]),
            copy(right, far_b.at[pl.ds(0, rows), :], sems.at[base + 1]),
        ]
    if j == 2:
        return [
            copy(left, far_a.at[pl.ds(rows, rows), :], sems.at[base + 2]),
            copy(right, b2b, sems.at[base + 3]),
        ]
    if j == 1:
        return [
            copy(left, b1a, sems.at[base + 4]),
            copy(right, far_b.at[pl.ds(rows, rows), :], sems.at[base + 5]),
        ]
    return [copy(buf.at[0], b0, sems.at[base + 6])]


def block_shapes(fw, cols, first_cols):
    rest = cols - first_cols
    sizes = [(4 * fw, first_cols), (4 * fw, rest), (2 * fw, first_cols), (2 * fw, rest), (2 * fw, cols)]
    return [jax.ShapeDtypeStruct(size, bf16) for size in sizes]


def feed_first(scal, a_src, g_src, w_gate, w_up, w_down, pieces, lo, hi, first_cols):
    length, D = segments_length(a_src), a_src[0].shape[1]
    dh = w_gate.shape[0]
    chips = lax.axis_size("dp") // 2
    hidden = w_gate.shape[1] // 2
    n = hi - lo
    fw = dh // chips
    arrays = unique_arrays(pieces)
    split = [clip_pieces(pieces, i * n, (i + 1) * n) for i in range(3)]
    blocks = chips == 4
    whole = len(a_src) > 1
    cols = 3 * n

    def kernel(scal_ref, *rest):
        a_refs, rest = rest[: len(a_src)], rest[len(a_src) :]
        g_refs, rest = rest[: len(g_src)], rest[len(g_src) :]
        wg_ref, wu_ref, wd_ref = rest[:3]
        piece_refs, rest = rest[3 : 3 + len(arrays)], rest[3 + len(arrays) :]
        d_ref, rest = rest[0], rest[1:]
        if blocks:
            far_a, far_b, b1a, b2b, b0 = rest[:5]
            rest = rest[5:]
        if whole:
            a_out, g_out = rest[:2]
            rest = rest[2:]
        a_buf, g_buf, wg, wu, wd, wdt, gate, up, buf, sems = rest
        e, k = scal_ref[0], scal_ref[1]
        start = pl.multiple_of(k * hidden + lo, 128)

        def copies(which):
            if which < 2:
                src, dst = ((wg_ref, wg), (wu_ref, wu))[which]
                own = pltpu.make_async_copy(
                    src.at[:, pl.ds(start, n)], dst.at[pl.ds(0, dh), :], sems.at[2 * which]
                )
                target = dst.at[pl.ds(dh, dh), :]
            else:
                own = pltpu.make_async_copy(wd_ref.at[pl.ds(start, n), :], wd, sems.at[4])
                target = wdt
            return [own] + piece_copies(
                split[which], arrays, piece_refs, target, e, fw, sems.at[2 * which + 1]
            )

        a_in = gather_tokens(a_refs, a_buf, sems.at[6])
        g_in = gather_tokens(g_refs, g_buf, sems.at[7])
        groups = [copies(i) for i in range(3)]
        start_all(a_in)
        start_all(groups[0])
        start_all(groups[1])
        start_all(g_in)
        start_all(groups[2])
        wait_all(a_in)
        wait_all(groups[0])
        for a, b in tiles_of(n, 256):
            gate[:, a:b] = mm(a_buf[...], wg[:, a:b])
        wait_all(groups[1])
        for a, b in tiles_of(n, 256):
            up[:, a:b] = mm(a_buf[...], wu[:, a:b])
        wait_all(g_in)
        wait_all(groups[2])
        for a, b in tiles_of(n, 256):
            dm = mm_t(g_buf[:, :dh], wd[a:b, :]) + mm(g_buf[:, dh:], wdt[:, a:b])
            gt, ut = gate[:, a:b], up[:, a:b]
            sig = jax.nn.sigmoid(gt)
            act = gt * sig
            d_ref[:, a:b] = (dm * ut * sig * (1.0 + gt * (1.0 - sig))).astype(bf16)
            d_ref[:, n + a : n + b] = (dm * act).astype(bf16)
            d_ref[:, 2 * n + a : 2 * n + b] = (act * ut).astype(bf16)
        outs = []
        if whole:
            outs += [
                pltpu.make_async_copy(a_buf, a_out, sems.at[8]),
                pltpu.make_async_copy(g_buf, g_out, sems.at[9]),
            ]
            start_all(outs)
        if blocks:

            def leave(j):
                return leave_block(buf, j, first_cols, (far_a, far_b, b1a, b2b, b0), sems, 10)

            def one(i, carry):
                j, h = 3 - i // 2, i % 2
                at = pl.ds(pl.multiple_of(h * dh + (e ^ j) * fw, fw), fw)
                rows = pl.ds(pl.multiple_of(h * fw, fw), fw)
                left = a_buf[:, at]
                buf[j, rows, : 2 * n] = t_mm(left, d_ref[:, : 2 * n]).astype(bf16)
                buf[j, rows, 2 * n :] = t_mm(g_buf[:, at], d_ref[:, 2 * n :]).astype(bf16)
                for jj in range(4):

                    @pl.when((j == jj) & (h == 1))
                    def _(jj=jj):
                        start_all(leave(jj))

                return carry

            lax.fori_loop(0, 8, one, 0)
            for j in range(4):
                outs += leave(j)
        wait_all(outs)

    full = lambda shape: pl.BlockSpec(shape, lambda i, s: (0,) * len(shape))
    out_shape, out_specs = [jax.ShapeDtypeStruct((length, cols), bf16)], [full((length, cols))]
    if blocks:
        out_shape += block_shapes(fw, cols, first_cols)
        out_specs += [ANY] * 5
    if whole:
        out_shape += [jax.ShapeDtypeStruct((length, D), bf16)] * 2
        out_specs += [ANY] * 2
    return pl.pallas_call(
        kernel,
        grid_spec=pltpu.PrefetchScalarGridSpec(
            num_scalar_prefetch=1,
            grid=(1,),
            in_specs=[ANY] * (len(a_src) + len(g_src) + 3 + len(arrays)),
            out_specs=out_specs,
            scratch_shapes=[
                pltpu.VMEM((length, D), bf16),
                pltpu.VMEM((length, D), bf16),
                pltpu.VMEM((D, n), bf16),
                pltpu.VMEM((D, n), bf16),
                pltpu.VMEM((n, dh), bf16),
                pltpu.VMEM((dh, n), bf16),
                pltpu.VMEM((length, n), f32),
                pltpu.VMEM((length, n), f32),
                pltpu.VMEM((4, 2 * fw, cols) if blocks else (1, 8, 128), bf16),
                pltpu.SemaphoreType.DMA((17,)),
            ],
        ),
        out_shape=out_shape,
        compiler_params=params(1),
        name="feed_first",
    )(scal, *a_src, *g_src, w_gate, w_up, w_down, *arrays)


def segments_length(sources):
    return sum(v.shape[0] for v in sources)


def feed_out(scal, kind, d, w_own, pieces, lo, hi, before, last):
    length = d.shape[0]
    n = hi - lo
    down = kind == "down"
    dh = w_own[0].shape[1] if down else w_own[0].shape[0]
    hidden = w_own[0].shape[0 if down else 1] // 2
    D = 2 * dh
    fw = dh // (lax.axis_size("dp") // 2)
    arrays = unique_arrays(pieces)
    ids = [2] if down else [0, 1]
    count = len(ids)
    split = [clip_pieces(pieces, i * n, (i + 1) * n) for i in ids]
    extra = [] if before is None else [before]

    def kernel(scal_ref, d_ref, *rest):
        own_refs, rest = rest[:count], rest[count:]
        piece_refs, rest = rest[: len(arrays)], rest[len(arrays) :]
        before_refs, rest = rest[: len(extra)], rest[len(extra) :]
        out_refs, rest = rest[: 2 if last else 1], rest[2 if last else 1 :]
        own_bufs, rest = rest[:count], rest[count:]
        oth_bufs, rest = rest[:count], rest[count:]
        d_buf, before_buf, sems = rest
        e, k = scal_ref[0], scal_ref[1]
        start = pl.multiple_of(k * hidden + lo, 128)
        own_copies, oth_copies = [], []
        for i in range(count):
            src = own_refs[i]
            src = src.at[pl.ds(start, n), :] if down else src.at[:, pl.ds(start, n)]
            own_copies.append(pltpu.make_async_copy(src, own_bufs[i], sems.at[2 * i]))
            oth_copies += piece_copies(
                split[i], arrays, piece_refs, oth_bufs[i], e, fw, sems.at[2 * i + 1]
            )
        d_copy = pltpu.make_async_copy(
            d_ref.at[:, pl.ds(ids[0] * n, count * n)], d_buf, sems.at[4]
        )
        d_copy.start()
        start_all(own_copies)
        before_copies = [pltpu.make_async_copy(ref, before_buf, sems.at[5]) for ref in before_refs]
        start_all(before_copies)
        start_all(oth_copies)
        d_copy.wait()

        def emit(value, a, b):
            if extra:
                value = value + before_buf[:, a:b]
            if last:
                split_store(value, out_refs[0], out_refs[1], slice(a, b))
            else:
                out_refs[0][:, a:b] = value

        wait_all(own_copies)
        wait_all(before_copies)
        for a, b in tiles_of(dh, 256):
            if down:
                value = mm(d_buf[...], own_bufs[0][:, a:b])
            else:
                value = mm_t(d_buf[:, :n], own_bufs[0][a:b, :])
                value = value + mm_t(d_buf[:, n:], own_bufs[1][a:b, :])
            emit(value, a, b)
        wait_all(oth_copies)
        for a, b in tiles_of(dh, 256):
            value = mm_t(d_buf[:, :n], oth_bufs[0][a:b, :])
            if not down:
                value = value + mm_t(d_buf[:, n:], oth_bufs[1][a:b, :])
            emit(value, dh + a, dh + b)

    full = lambda shape: pl.BlockSpec(shape, lambda i, s: (0,) * len(shape))
    half = (length // 2, D)
    if last:
        out_shape = [jax.ShapeDtypeStruct(half, bf16), jax.ShapeDtypeStruct(half, f32)]
    else:
        out_shape = [jax.ShapeDtypeStruct((length, D), f32)]
    own_shape = (n, dh) if down else (dh, n)
    out = pl.pallas_call(
        kernel,
        grid_spec=pltpu.PrefetchScalarGridSpec(
            num_scalar_prefetch=1,
            grid=(1,),
            in_specs=[ANY] * (1 + count + len(arrays) + len(extra)),
            out_specs=[full(v.shape) for v in out_shape],
            scratch_shapes=[pltpu.VMEM(own_shape, bf16)] * count
            + [pltpu.VMEM((dh, n), bf16)] * count
            + [
                pltpu.VMEM((length, count * n), bf16),
                pltpu.VMEM((length, D) if extra else (8, 128), f32),
                pltpu.SemaphoreType.DMA((6,)),
            ],
        ),
        out_shape=out_shape,
        compiler_params=params(1),
    )(scal, d, *w_own, *arrays, *extra)
    return out if last else out[0]


def attend_grads(scal, groups, first_cols):
    _, D = groups[0][0].shape
    dh = D // 2
    fw = dh // 4
    lefts = []
    for left, _ in groups:
        if not any(left is v for v in lefts):
            lefts.append(left)
    picks = [[left is v for v in lefts].index(True) for left, _ in groups]
    rights = [right for _, right in groups]
    cols = sum(v.shape[1] for v in rights)

    def kernel(scal_ref, *rest):
        left_refs, rest = rest[: len(lefts)], rest[len(lefts) :]
        right_refs, rest = rest[: len(rights)], rest[len(rights) :]
        outs, (buf, sems) = rest[:5], rest[5:]
        e = scal_ref[0]

        def leave(j):
            return leave_block(buf, j, first_cols, outs, sems, 0)

        def one(i, carry):
            j, h = 3 - i // 2, i % 2
            at = pl.ds(pl.multiple_of(h * dh + (e ^ j) * fw, fw), fw)
            rows = pl.ds(pl.multiple_of(h * fw, fw), fw)
            col = 0
            for pick_at, right in zip(picks, right_refs):
                width = right.shape[1]
                value = t_mm(left_refs[pick_at][:, at], right[...]).astype(bf16)
                buf[j, rows, col : col + width] = value
                col += width
            for jj in range(4):

                @pl.when((j == jj) & (h == 1))
                def _(jj=jj):
                    start_all(leave(jj))

            return carry

        lax.fori_loop(0, 8, one, 0)
        for j in range(4):
            wait_all(leave(j))

    full = lambda shape: pl.BlockSpec(shape, lambda i, s: (0,) * len(shape))
    return pl.pallas_call(
        kernel,
        grid_spec=pltpu.PrefetchScalarGridSpec(
            num_scalar_prefetch=1,
            grid=(1,),
            in_specs=[full(v.shape) for v in lefts + rights],
            out_specs=[ANY] * 5,
            scratch_shapes=[
                pltpu.VMEM((4, 2 * fw, cols), bf16),
                pltpu.SemaphoreType.DMA((7,)),
            ],
        ),
        out_shape=block_shapes(fw, cols, first_cols),
        compiler_params=params(1),
        name="attend_grads",
    )(scal, *lefts, *rights)


def widen(v):
    return v.astype(f32)


def reduce_blocks(scal, blocks, first_cols, split=False):
    far_a, far_b, b1a, b2b, b0 = blocks
    rows = b0.shape[0]
    fw = rows // 2
    got_a = swap_chip(far_a, 1)
    got_b = swap_chip(far_b, 0)
    to_x = (widen(b1a) + widen(got_a[:rows])).astype(bf16)
    to_y = (widen(b2b) + widen(got_b[:rows])).astype(bf16)
    got_x = swap_chip(to_x, 0)
    got_y = swap_chip(to_y, 1)

    held = lax.optimization_barrier((b0, got_a, got_b, got_x, got_y))
    oth = sum_blocks(held, first_cols, slice(fw, rows), bf16)
    got_z = swap_row(oth)
    if split:
        return finish_span(scal, (b0, got_a, got_b, got_x, got_y, got_z), first_cols)
    parts = lax.optimization_barrier((b0, got_a, got_b, got_x, got_y, got_z))
    return sum_blocks(parts, first_cols, slice(0, fw), f32) + widen(parts[5])


def finish_span(scal, parts, first_cols):
    b0 = parts[0]
    cols = b0.shape[1]
    fw, n = b0.shape[0] // 2, cols // 3
    half = fw // 2

    def kernel(scal_ref, b0_ref, a_ref, b_ref, x_ref, y_ref, z_ref, mine_ref, theirs_ref, down_ref, total):
        k = scal_ref[1]
        total[:, :first_cols] = widen(b0_ref[:, :first_cols]) + widen(a_ref[...]) + widen(x_ref[...])
        total[:, first_cols:] = widen(b0_ref[:, first_cols:]) + widen(b_ref[...]) + widen(y_ref[...])
        total[...] += widen(z_ref[...])
        here = pl.ds(pl.multiple_of(k * half, half), half)
        away = pl.ds(pl.multiple_of((1 - k) * half, half), half)
        mine_ref[...] = total[here, : 2 * n]
        theirs_ref[...] = total[away, : 2 * n]
        down_ref[...] = total[:, 2 * n :].astype(bf16)

    def rows(v, at):
        return pl.BlockSpec((fw, v.shape[1]), lambda i, s: (at, 0))

    full = lambda shape: pl.BlockSpec(shape, lambda i, s: (0,) * len(shape))
    out_shape = [
        jax.ShapeDtypeStruct((half, 2 * n), f32),
        jax.ShapeDtypeStruct((half, 2 * n), f32),
        jax.ShapeDtypeStruct((fw, n), bf16),
    ]
    return pl.pallas_call(
        kernel,
        grid_spec=pltpu.PrefetchScalarGridSpec(
            num_scalar_prefetch=1,
            grid=(1,),
            in_specs=[rows(v, at) for v, at in zip(parts, (0, 2, 2, 0, 0, 0))],
            out_specs=[full(v.shape) for v in out_shape],
            scratch_shapes=[pltpu.VMEM((fw, cols), f32)],
        ),
        out_shape=out_shape,
        compiler_params=params(1),
        name="finish_span",
    )(scal, *parts)


def join_spans(scal, spans, mine, theirs):
    hidden = sum(v.shape[1] for v in mine) // 2
    count = len(spans)

    def kernel(scal_ref, *rest):
        outs, sems = rest[2 * count : 2 * count + 2], rest[-1]
        k = scal_ref[1]
        copies = []
        for side in range(2):
            core = k if side == 0 else 1 - k
            for i, (lo, hi) in enumerate(spans):
                ref, n = rest[side * count + i], hi - lo
                at = pl.ds(pl.multiple_of(core * hidden + lo, 128), n)
                for which in range(2):
                    copies.append(
                        pltpu.make_async_copy(
                            ref.at[:, pl.ds(which * n, n)],
                            outs[which].at[:, at],
                            sems.at[len(copies)],
                        )
                    )
        start_all(copies)
        wait_all(copies)

    full = lambda shape: pl.BlockSpec(shape, lambda i, s: (0,) * len(shape))
    shape = jax.ShapeDtypeStruct((mine[0].shape[0], 2 * hidden), f32)
    return pl.pallas_call(
        kernel,
        grid_spec=pltpu.PrefetchScalarGridSpec(
            num_scalar_prefetch=1,
            grid=(1,),
            in_specs=[full(v.shape) for v in mine + theirs],
            out_specs=[ANY] * 2,
            scratch_shapes=[pltpu.SemaphoreType.DMA((4 * count,))],
        ),
        out_shape=[shape] * 2,
        compiler_params=params(1),
        name="join_spans",
    )(scal, *mine, *theirs)


def sum_blocks(parts, first_cols, part, kind):
    b0, got_a, got_b, got_x, got_y = parts[:5]
    rows = b0.shape[0]
    left = widen(b0[part, :first_cols]) + widen(got_a[rows:][part]) + widen(got_x[part])
    right = widen(b0[part, first_cols:]) + widen(got_b[rows:][part]) + widen(got_y[part])
    return jnp.concatenate([left.astype(kind), right.astype(kind)], 1)


def reduce_groups(e, groups):
    chips = lax.axis_size("dp") // 2
    nbits = chips.bit_length() - 1
    dh = groups[0][0].shape[1] // 2

    def make(keys):
        outs = []
        for left, right in groups:
            left = jnp.concatenate(
                [xor_axis(left[:, :dh], e, 1, chips), xor_axis(left[:, dh:], e, 1, chips)], 1
            )
            left = take_keys(left, list(range(chips)), keys, 1)
            outs.append(t_mm(left, right))
        return jnp.concatenate(outs, 1)

    return reduce_features(make, list(range(nbits)), 0)


def tp_finish(send, keep):
    got = swap_core(send)
    half = keep.shape[0] // 2
    away = (keep[half:] + widen(got[half:])).astype(bf16)
    mate = swap_col(away)
    return keep[:half] + widen(got[:half]) + widen(mate)


def on_device(
    tokens,
    segments,
    positions,
    attn_gain,
    w_query,
    w_key,
    w_value,
    w_out,
    mlp_gain,
    w_gate,
    w_up,
    w_down,
    cotangent,
):
    dp = lax.axis_index("dp")
    e, k = dp >> 1, dp & 1
    r, c = lax.axis_index("row"), lax.axis_index("col")
    chips = lax.axis_size("dp") // 2
    nbits = chips.bit_length() - 1
    scal = jnp.stack([e, k, c]).astype(jnp.int32)
    diag = k == r
    length = segments.shape[1]
    blk = length // 4
    dh = tokens.shape[2]
    D = 2 * dh
    fw = dh // chips
    nq = w_query.shape[1] // 2
    hidden = w_gate.shape[1] // 2
    first, second = side_perms()

    def spread_in(v):
        parts = v[0].reshape(2, blk, dh)
        here = jnp.where(r == 0, parts[0], parts[1])
        away = jnp.where(r == 0, parts[1], parts[0])
        here, away = lax.optimization_barrier((here, away))
        got_a = lax.ppermute(away, ("dp", "row"), first)
        got_b = lax.ppermute(here, ("dp", "row"), second)
        own = jnp.where(diag, here, got_a)
        oth = jnp.where(diag, got_a, got_b)
        return jnp.concatenate([own, oth], 1)

    def spread_out(v):
        own, oth = v[:, :dh], v[:, dh:]
        mixed = jnp.where(diag, oth, own)
        own, oth, mixed = lax.optimization_barrier((own, oth, mixed))
        got_a = lax.ppermute(mixed, ("dp", "row"), flip(first))
        got_b = lax.ppermute(oth, ("dp", "row"), flip(second))

        here = jnp.where(diag, own, got_b)
        return order_pair(here, got_a, r, 0)[None]

    gains = jnp.stack([attn_gain, mlp_gain])
    got_gains = swap_row(gains)
    meta = jnp.concatenate([segments, positions], 0)
    meta = jnp.where(diag, meta, swap_core(meta))
    marks_t = meta[:1]
    marks = marks_t.T
    quarter = jnp.split(meta[1:], 4, 1)
    order = xor_blocks([quarter[0], quarter[2], quarter[1], quarter[3]], 2 * k + c)
    place = jnp.concatenate(order, 1)[0]
    half = HD // 2
    frequency = 10000.0 ** (-jnp.arange(half, dtype=f32) * 2.0 / HD)
    angles = place.astype(f32)[:, None] * frequency[None, :]
    cosine, sine = jnp.cos(angles), jnp.sin(angles)
    cosine = jnp.concatenate([cosine] * 4, 1)
    sine = jnp.concatenate([-sine, sine] * 2, 1)

    x = spread_in(tokens)
    wkv = jnp.concatenate([pick(w_key, k, 1), pick(w_value, k, 1)], 1)

    def rows_shard(w, start, size):
        return lax.dynamic_slice(w, (e * fw, start), (fw, size))

    def cols_shard(w, start, size):
        return lax.dynamic_slice(w, (start, e * fw), (size, fw)).T

    parts = [rows_shard(w_query, k * nq, nq), rows_shard(wkv, 0, 128), cols_shard(w_out, k * nq, nq)]
    shard = jnp.concatenate(parts, 1)
    attn_pieces = gather_unit(swap_row(shard), 640)
    g = spread_in(cotangent)
    spans = [(0, 512), (512, 1024), (1024, hidden)]
    feed_pieces = []
    for lo, hi in spans:
        n = hi - lo
        at = k * hidden + lo
        parts = [rows_shard(w_gate, at, n), rows_shard(w_up, at, n), cols_shard(w_down, at, n)]
        groups = [(parts, 0)]
        pieces = []
        for group, col in groups:
            group = lax.optimization_barrier(group)
            shard = jnp.concatenate(group, 1)
            cut_at = shard.shape[1] // 256 * 128
            pieces += gather_unit(swap_row(shard), cut_at, col)
        feed_pieces.append(pieces)

    x, got_gains, gains = lax.optimization_barrier((x, got_gains, gains))
    gains = jnp.concatenate([gains, got_gains], 1)
    xf = x.astype(f32)
    r1 = lax.rsqrt(jnp.sum(xf * xf, axis=1, keepdims=True) / D + epsilon)
    a1 = (xf * r1 * gains[0]).astype(bf16)
    a1 = tp_gather(a1)
    q, kdup, vdup, o, send, keep, a1 = attend_forward(
        scal, a1, w_query, wkv, w_out, attn_pieces, cosine, sine, marks, marks_t
    )
    hres = xf + tp_finish(send, keep)
    r2 = lax.rsqrt(jnp.sum(hres * hres, axis=1, keepdims=True) / D + epsilon)
    a2 = (hres * r2 * gains[1]).astype(bf16)
    a2 = tp_gather(a2)
    g_all = tp_gather(g)

    out_part, da2_part = None, None
    feed_sums = []
    for i, ((lo, hi), pieces) in enumerate(zip(spans, feed_pieces)):
        last = i == len(spans) - 1
        n = hi - lo
        cut_at = 3 * n // 256 * 128
        outs = feed_first(scal, a2, g_all, w_gate, w_up, w_down, pieces, lo, hi, cut_at)
        d, outs = outs[0], outs[1:]
        if i == 0:
            a2, g_all = [outs[-2]], [outs[-1]]
        da2_part = feed_out(scal, "in", d, [w_gate, w_up], pieces, lo, hi, da2_part, last)
        if chips == 4:
            feed_sums.append(reduce_blocks(scal, outs[:5], cut_at, True))
        else:
            groups = [(a2[0], d[:, : 2 * n]), (g_all[0], d[:, 2 * n :])]
            feed_sums.append(reduce_groups(e, groups))
        out_part = feed_out(scal, "down", d, [w_down], pieces, lo, hi, out_part, last)
    kept, sent, keep = lax.optimization_barrier((hres, *out_part))
    result = tp_finish(sent, keep)
    result = (kept + result).astype(bf16)
    result = spread_out(result)

    def norm_back(inputs, factor, gain, upstream):
        weighted = upstream * gain
        dotted = jnp.sum(weighted * inputs, axis=1, keepdims=True)
        grad = factor * weighted - inputs * factor**3 * dotted / D
        return grad, jnp.sum(upstream * inputs * factor, axis=0)

    da2 = tp_finish(*da2_part)
    dh_grad, gain_two = norm_back(hres, r2, gains[1], da2)
    dh_grad = dh_grad + widen(g)
    dz = dh_grad.astype(bf16)
    dz = tp_gather(dz)
    dq, dkv, send, keep, dz = attend_backward(
        scal, dz, q, kdup, vdup, w_query, wkv, w_out, attn_pieces, cosine, sine, marks, marks_t
    )
    if chips == 4:
        o_blocks = attend_grads(scal, [(dz, o)], 256)
        q_blocks = attend_grads(scal, [(a1, dq), (a1, dkv)], 256)
        out_sum = reduce_blocks(scal, o_blocks, 256)
        qkv_sum = reduce_blocks(scal, q_blocks, 256)
    else:
        attn_sum = reduce_groups(e, [(a1, jnp.concatenate([dq, dkv], 1)), (dz, o)])
        qkv_sum, out_sum = attn_sum[:, : nq + 128], attn_sum[:, nq + 128 :]
    da1 = tp_finish(send, keep)
    grad_x, gain_one = norm_back(xf, r1, gains[0], da1)
    grad_x = (grad_x + dh_grad).astype(bf16)
    grad_x = spread_out(grad_x)

    both = jnp.stack([gain_one, gain_two])
    both = both + swap_core(both)
    for bit in range(nbits):
        both = both + swap_chip(both, bit)
    both = both + swap_col(both)
    own = both[:, :dh] + swap_row(both[:, dh:])

    def rows_home(v):
        return pick(v, k, 0), swap_core(pick(v, 1 - k, 0))

    if chips == 4:
        mines = [v[0] for v in feed_sums]
        others = [swap_core(v[1]) for v in feed_sums]
        grad_gate, grad_up = join_spans(scal, spans, mines, others)
        downs = [v[2] for v in feed_sums]
    else:
        homes = []
        for (lo, hi), v in zip(spans, feed_sums):
            homes.append(rows_home(v[:, : 2 * (hi - lo)]))
        grads = []
        for which in range(2):
            sides = []
            for side in range(2):
                for (lo, hi), home in zip(spans, homes):
                    n = hi - lo
                    sides.append(home[side][:, which * n : (which + 1) * n])
            mine = jnp.concatenate(sides[: len(spans)], 1)
            theirs = jnp.concatenate(sides[len(spans) :], 1)
            grads.append(order_pair(mine, theirs, k, 1))
        grad_gate, grad_up = grads
        downs = [v[:, 2 * (hi - lo) :] for (lo, hi), v in zip(spans, feed_sums)]
    mine, theirs = rows_home(qkv_sum)
    grad_query = order_pair(mine[:, :nq], theirs[:, :nq], k, 1)
    grad_key = order_pair(mine[:, nq : nq + HD], theirs[:, nq : nq + HD], k, 1)
    grad_value = order_pair(mine[:, nq + HD :], theirs[:, nq + HD :], k, 1)

    def exchange(sums):
        views = []
        for v in sums:
            v = v.astype(bf16).T
            views.append(v.reshape(chips // 2, 2, v.shape[0] // chips, v.shape[1]))
        view = jnp.concatenate(views, 2)
        mine = jnp.where(k == 0, view[:, 0], view[:, 1])
        got = swap_core(jnp.where(k == 0, view[:, 1], view[:, 0]))
        full = order_pair(mine, got, k, 0)
        rel = xor_blocks([full[i] for i in range(chips)], e)
        n = lax.axis_size("dp")
        out = [rel[0]]
        for j in range(1, chips):
            out.append(lax.ppermute(rel[j], "dp", [(i, i ^ (2 * j)) for i in range(n)]))
        cut_at = views[0].shape[2]
        whole = xor_blocks(out, e)
        return [
            jnp.concatenate([v[part] for v in whole], 1).astype(f32)
            for part in (slice(0, cut_at), slice(cut_at, None))
        ]

    grad_down, grad_out = exchange([jnp.concatenate(downs, 1), out_sum])
    return (
        result,
        grad_x,
        own[0],
        grad_query[None],
        grad_key[None],
        grad_value[None],
        grad_out[None],
        own[1],
        grad_gate[None],
        grad_up[None],
        grad_down[None],
    )


def solution(mesh):
    placed = (
        P("dp", "col", "row"),
        P("dp", None),
        P("dp", None),
        P("row"),
        P("row", "col"),
        P("row", "col"),
        P("row", "col"),
        P("col", "row"),
        P("row"),
        P("row", "col"),
        P("row", "col"),
        P("col", "row"),
        P("dp", "col", "row"),
    )
    return jax.shard_map(
        on_device,
        mesh=mesh,
        in_specs=placed,
        out_specs=(
            P("dp", "col", "row"),
            P("dp", "col", "row"),
            P("row"),
            P("row", "dp", "col"),
            P("row", "dp", "col"),
            P("row", "dp", "col"),
            P("col", "dp", "row"),
            P("row"),
            P("row", "dp", "col"),
            P("row", "dp", "col"),
            P("col", "dp", "row"),
        ),
        check_vma=False,
    )
```
